32 devices in a mesh: dp: 8 (over z, y), mp: 4 (over x, core).
Axes of the slice: x: 2, y: 2, z: 4, core: 2. Of those that a mesh axis runs over, the one named last changes fastest.
Arguments:
- token_pool: bfloat16 [4096, 3072], P('dp'), may hold values from -6 to 6
- visible: int32 [1024], P('dp'), may hold values from 0 to 511, as said below
- out_grad: bfloat16 [1024, 3072], P('dp'), may hold values from -2.5 to 2.5
- ln_gain: float32 [3072], replicated, may hold values from 0.5 to 1.5
- master_up: float32 [3072, 12288], P('dp', 'mp'), may hold values from -0.109375 to 0.109375
- master_down: float32 [3072, 12288], P('dp', 'mp'), may hold values from -0.0546875 to 0.0546875
- row_up: float32 [3072], P('dp'), may hold values from 0.02 to 5
- col_up: float32 [12288], P('mp'), may hold values from 0.05 to 0.5
- row_down: float32 [3072], P('dp'), may hold values from 0.02 to 5
- col_down: float32 [12288], P('mp'), may hold values from 0.05 to 0.5
Outputs:
- update_up: float32 [3072, 12288], P('dp', 'mp')
- update_down: float32 [3072, 12288], P('dp', 'mp')
- row_up_new: float32 [3072], P('dp')
- col_up_new: float32 [12288], P('mp')
- row_down_new: float32 [3072], P('dp')
- col_down_new: float32 [12288], P('mp')
The draws below stay inside these ranges and needn't reach their ends.
Inputs may be any that keep to these rules, and one draw needn't show every extreme that they name: `visible`: each aligned block of 128 entries lists distinct patch indices of that block's 512 patches, in rising order.
All inputs are finite; a program needn't handle non-finite values.
Results may differ from the reference program's by a relative error of at most 0.0059.
Values may be sent and summed in bfloat16 or wider, within the bound.
A program may use at most 256 MiB of HBM per device.

```python
import math
import jax
import jax.numpy as jnp
from jax import lax

D = 3072
FF = 12288
TOK_DEV = 128
ALL_DEV = 512
TOKENS = 1024
POOL = 4096


def draw_visible(key, part):
    blocks = TOKENS // TOK_DEV
    keys = jax.random.split(jax.random.fold_in(key, 17), blocks)
    orders = jax.vmap(lambda one_key: jax.random.permutation(one_key, ALL_DEV))(keys)
    chosen = jnp.sort(orders[:, :TOK_DEV], axis=1)
    return chosen.reshape(-1).astype(jnp.int32)


def rising_factor(key, salt):
    place = jnp.arange(D, dtype=jnp.float32) / max(D - 1, 1)
    jitter = jnp.exp(jax.random.uniform(jax.random.fold_in(key, salt), (D,), jnp.float32, -0.35, 0.35))
    base = 0.05 * jnp.exp(place * jnp.log(40.0))
    return (base * jitter).astype(jnp.float32)


def draw_row_up(key, part):
    return rising_factor(key, 31)


def draw_row_down(key, part):
    return rising_factor(key, 47)


def strengthened(array, rng, source, target, parts, factor):
    def block_of(dim):
        return (jnp.arange(array.shape[dim]) // (array.shape[dim] // parts)).reshape((-1,) + (1,) * (array.ndim - 1 - dim))

    one_side = jax.random.permutation(rng, parts)[block_of(target)]
    far = (block_of(target) + parts // 2) % parts
    return jnp.where((block_of(source) == one_side) | (block_of(source) == far), factor * array, array)


def shard_levels(rng, dims, pieces, least, largest):
    def one(axis_at, parts):
        heights = jax.random.uniform(jax.random.fold_in(jax.random.fold_in(rng, 6), axis_at), (parts,), jnp.float32, least / len(pieces), largest / len(pieces))
        return jnp.repeat(jnp.exp(heights), dims[axis_at] // parts).reshape((-1,) + (1,) * (len(dims) - axis_at - 1))

    level = one(*pieces[0])
    for cut in pieces[1:]:
        level = level * one(*cut)
    return level


def bell_draw(own_key, dims, width, reach, shards=(), kind=jnp.bfloat16):
    array = jax.random.normal(own_key, dims, jnp.float32) * width
    if len(shards) > 0:
        array = shard_levels(own_key, dims, shards, -0.22, 0.18) * array
    return jnp.clip(array, min=-reach, max=reach).astype(kind)


def noise_with(key, shape, deviation, reach, cuts, heavy, kind=jnp.bfloat16):
    entries = deviation * jax.random.normal(key, shape, jnp.float32)
    if cuts:
        entries = entries * shard_levels(key, shape, cuts, -0.22, 0.18)
    return jnp.clip(strengthened(entries, jax.random.fold_in(key, 3), *heavy), -reach, reach).astype(kind)


def setup_inputs(seed: int = 0) -> dict:
    arg_keys = jax.random.split(jax.random.key(seed), 11)
    token_pool = noise_with(arg_keys[0], (POOL, D), 1.0, 6.0, ((0, 8),), (0, 1, 8, 2.0))
    visible = draw_visible(jax.random.fold_in(arg_keys[10], 71), 0)
    out_grad = noise_with(arg_keys[2], (TOKENS, D), (4.0 * TOKENS ** -0.5), 2.5, ((0, 8),), (0, 1, 8, 2.0))
    ln_gain = jnp.clip(1.0 + 0.1 * jax.random.normal(arg_keys[3], (D,), jnp.float32), 0.5, 1.5)
    master_up = bell_draw(arg_keys[4], (D, FF), D ** -0.5, 0.109375, ((0, 8), (1, 4)), jnp.float32)
    master_down = bell_draw(arg_keys[5], (D, FF), FF ** -0.5, 0.0546875, ((0, 8), (1, 4)), jnp.float32)
    row_up = draw_row_up(jax.random.fold_in(arg_keys[10], 71), 0)
    col_up = jnp.clip(jnp.exp(math.log(0.5) - 2.3025851 * jax.random.uniform(arg_keys[7], (FF,), jnp.float32) ** shard_levels(arg_keys[7], (FF,), ((0, 4),), -0.2, 0.2)), 0.05, 0.5)
    row_down = draw_row_down(jax.random.fold_in(arg_keys[10], 71), 0)
    col_down = jnp.clip(jnp.exp(math.log(0.5) - 2.3025851 * jax.random.uniform(arg_keys[9], (FF,), jnp.float32) ** shard_levels(arg_keys[9], (FF,), ((0, 4),), -0.2, 0.2)), 0.05, 0.5)
    return {"token_pool": token_pool, "visible": visible, "out_grad": out_grad, "ln_gain": ln_gain, "master_up": master_up, "master_down": master_down, "row_up": row_up, "col_up": col_up, "row_down": row_down, "col_down": col_down}


decay_rate = 0.8
norm_eps = 1e-06
tiny_value = 1e-30

def gelu_tanh(values):
    return jax.nn.gelu(values, approximate=True)

def normalize(values, gain):
    mean_val = lax.optimization_barrier(jnp.mean(values, axis=1, keepdims=True))
    centred = values - mean_val
    variance = lax.optimization_barrier(jnp.mean(centred * centred, axis=1, keepdims=True))
    return (centred * lax.rsqrt(variance + norm_eps) * gain).astype(jnp.bfloat16)

def contract_tokens(left, right):
    return lax.dot_general(left, right, (((0,), (0,)), ((), ())), preferred_element_type=jnp.float32)

def factored_update(grad, row_old, col_old):
    squares = grad * grad + tiny_value
    row_new = decay_rate * row_old + (1.0 - decay_rate) * lax.optimization_barrier(jnp.mean(squares, axis=1))
    col_new = decay_rate * col_old + (1.0 - decay_rate) * lax.optimization_barrier(jnp.mean(squares, axis=0))
    raw = grad * lax.rsqrt(row_new[:, None] * col_new[None, :])
    spread = jnp.sqrt(jnp.mean(raw * raw))
    return (raw / jnp.maximum(1.0, spread), row_new, col_new)

def reference(token_pool, visible, out_grad, ln_gain, master_up, master_down, row_up, col_up, row_down, col_down):
    owner = jnp.arange(visible.shape[0], dtype=jnp.int32) // TOK_DEV * ALL_DEV
    picked = token_pool[(visible + owner).astype(jnp.int32)].astype(jnp.float32)
    normed = normalize(picked, ln_gain)
    w_up = master_up.astype(jnp.bfloat16)
    w_down = master_down.astype(jnp.bfloat16)
    pre_act = jnp.dot(normed, w_up, preferred_element_type=jnp.float32)
    act_value, pull_back = jax.vjp(gelu_tanh, pre_act)
    hidden_act = act_value.astype(jnp.bfloat16)
    act_grad = jnp.dot(out_grad, w_down, preferred_element_type=jnp.float32)
    pre_grad = pull_back(act_grad)[0].astype(jnp.bfloat16)
    grad_up = contract_tokens(normed, pre_grad)
    grad_down = contract_tokens(out_grad, hidden_act)
    update_up, row_up_new, col_up_new = factored_update(grad_up, row_up, col_up)
    update_down, row_down_new, col_down_new = factored_update(grad_down, row_down, col_down)
    return (update_up, update_down, row_up_new, col_up_new, row_down_new, col_down_new)
```

```python
import functools
import jax
import jax.numpy as jnp
from jax import lax
from jax.experimental import pallas as pl
from jax.experimental.pallas import tpu as pltpu
from jax.sharding import PartitionSpec as P

decay_rate = 0.8
norm_eps = 1e-06
tiny_value = 1e-30


def gelu_tanh(values):
    return jax.nn.gelu(values, approximate=True)


def normalize(values, gain):
    mean_val = jnp.mean(values, axis=1, keepdims=True)
    centred = values - mean_val
    variance = jnp.mean(centred * centred, axis=1, keepdims=True)
    return (centred * lax.rsqrt(variance + norm_eps) * gain).astype(jnp.bfloat16)


def contract_tokens(left, right):
    return lax.dot_general(
        left, right, (((0,), (0,)), ((), ())), preferred_element_type=jnp.float32
    )


def finish_update(grad, row_new, col_new):
    return grad * lax.rsqrt(row_new[:, None] * col_new[None, :])


def gathered_grads(normed, out_grad, w_up, w_down):
    left = normed
    pre_act = jnp.dot(
        left, lax.all_gather(w_up, "dp", axis=0, tiled=True), preferred_element_type=jnp.float32
    )
    act_value, pull_back = jax.vjp(gelu_tanh, pre_act)
    hidden_act = act_value.astype(jnp.bfloat16)
    left = out_grad
    act_grad = jnp.dot(
        left, lax.all_gather(w_down, "dp", axis=0, tiled=True), preferred_element_type=jnp.float32
    )
    pre_grad = pull_back(act_grad)[0].astype(jnp.bfloat16)
    grad_down = lax.psum_scatter(
        contract_tokens(out_grad, hidden_act), "dp", scatter_dimension=0, tiled=True
    )
    grad_up = lax.psum_scatter(
        contract_tokens(normed, pre_grad), "dp", scatter_dimension=0, tiled=True
    )
    return grad_up, grad_down


MESH = pl.DeviceIdType.MESH


def flipped(index):
    return index + 1 - 2 * lax.rem(index, 2)


def greet(devices):
    barrier = pltpu.get_barrier_semaphore()
    for device in devices:
        pl.semaphore_signal(barrier, inc=1, device_id=device, device_id_type=MESH)
    pl.semaphore_wait(barrier, len(devices))


def send(src, dst, send_sem, recv_sem, device):
    return pltpu.make_async_remote_copy(
        src_ref=src,
        dst_ref=dst,
        send_sem=send_sem,
        recv_sem=recv_sem,
        device_id=device,
        device_id_type=MESH,
    )


def block_step_kernel(
    sizes,
    pool,
    visible,
    out_grad,
    gain,
    master_up,
    master_down,
    row_up,
    row_down,
    col_up,
    col_down,
    grads,
    row_new,
    col_new,
    energy,
    pool_buf,
    picked,
    acts,
    left,
    left_t,
    masters,
    cast_out,
    weights,
    partial,
    crossing,
    hidden,
    grad_buf,
    col_parts,
    col_halves,
    inverse,
    row_acc,
    spent_acc,
    stats,
    stat_buf,
    energy_buf,
    local_sem,
    master_sem,
    lev_send,
    lev_recv,
    act_send,
    act_recv,
    weight_send,
    weight_recv,
    part_send,
    part_recv,
    cross_recv,
    hid_send,
    hid_recv,
    grad_send,
    grad_recv,
    store_sem,
    col_send,
    col_recv,
    half_send,
    half_recv,
    stat_send,
    stat_recv,
    energy_send,
    energy_recv,
):
    chunks, width, groups, lag = sizes
    me = lax.axis_index("dp")
    col = lax.axis_index("mp")
    z = lax.div(me, 2)
    y = lax.rem(me, 2)
    inner = jnp.logical_or(z == 1, z == 2)
    outer = jnp.logical_not(inner)
    rows = master_up.shape[0]
    half = master_up.shape[1] // 2
    depth = rows * 8
    breadth = master_up.shape[1] * 4
    deep = 2 * rows
    part = out_grad.shape[0] // 4
    group = 8 * part
    units = chunks * groups
    mine = y * 4 + col
    beside = flipped(me)
    core = flipped(col)
    across = lax.rem(col + 2, 4)
    inward = me + jnp.where(z < 2, 2, -2)
    outward = me - jnp.where(z < 2, 2, -2)
    masters_in = (master_up, master_down)
    peers = [lax.rem(me + shift, 8) for shift in range(1, 8)]
    level = [lax.rem(mine + shift, 8) for shift in range(1, 8)]

    def level_device(index):
        return (z * 2 + lax.div(index, 4), lax.rem(index, 4))

    def row_block(index, size):
        return pl.ds(pl.multiple_of(index * size, size), size)

    load_pool = pltpu.make_async_copy(pool, pool_buf, local_sem.at[0])
    load_out = pltpu.make_async_copy(out_grad.at[row_block(col, part)], acts.at[1], local_sem.at[1])

    def master_loads(k):
        copies = []
        for a in range(2):
            for side in range(2):
                owner = y if side == 0 else 1 - y
                cols = pl.ds(pl.multiple_of(owner * half + k * width, width), width)
                copies.append(
                    pltpu.make_async_copy(
                        masters_in[a].at[:, cols], masters.at[k, a, side], master_sem.at[k, 2 * a + side]
                    )
                )
        return copies

    def start_loads(k):
        for copy in master_loads(k):
            copy.start()

    start_loads(0)
    load_pool.start()
    load_out.start()

    @pl.loop(1, chunks)
    def _(k):
        start_loads(k)

    greet(
        [(other, col) for other in peers]
        + [(me, lax.rem(col + shift, 4)) for shift in range(1, 4)]
        + [(beside, lax.rem(col + shift, 4)) for shift in range(1, 4)]
    )

    my_rows = row_block(y, rows)

    def weight_copy(k):
        return send(
            cast_out.at[k], weights.at[k, :, my_rows], weight_send.at[k], weight_recv.at[k], (beside, col)
        )

    def cast_chunk(k):
        for copy in master_loads(k):
            copy.wait()
        for a in range(2):
            cast_out[k, a] = masters[k, a, 1].astype(jnp.bfloat16)
        weight_copy(k).start()
        for a in range(2):
            weights[k, a, my_rows] = masters[k, a, 0].astype(jnp.bfloat16)

    cast_chunk(0)
    row_acc[...] = jnp.zeros_like(row_acc)
    spent_acc[...] = jnp.zeros_like(spent_acc)

    load_pool.wait()
    places = lax.broadcasted_iota(jnp.int32, (pool.shape[0], out_grad.shape[0]), 0)
    chosen = (places == visible[...]).astype(jnp.bfloat16)
    for level_at in range(4):
        span = pl.ds(level_at * deep, deep)
        picked[:, span] = contract_tokens(chosen, pool_buf[:, span])
    acts[0] = normalize(picked[row_block(col, part), :], gain[...])
    load_out.wait()

    def place(owner):
        return jnp.where(owner == 0, 2, jnp.where(owner == 1, 0, jnp.where(owner == 2, 1, 3)))

    def piece(owner, index):
        return left.at[:, pl.ds(pl.multiple_of(place(owner) * group + index * part, part), part)]

    lev_copies = []
    for shift in (1, 3, 2):
        to = lax.rem(z + shift, 4)
        copy = send(
            acts.at[:, :, pl.ds(pl.multiple_of(to * deep, deep), deep)],
            piece(z, mine),
            lev_send.at[shift - 1],
            lev_recv.at[shift - 1],
            (to * 2 + y, col),
        )
        copy.start()
        lev_copies.append((shift, copy))
    piece(z, mine)[...] = acts[:, :, pl.ds(pl.multiple_of(z * deep, deep), deep)]

    other_mine = (1 - y) * 4 + col
    mine_across = y * 4 + across
    other_across = (1 - y) * 4 + across
    act_copies = []

    def share(owner, index, slot, kind, device):
        copy = send(
            piece(owner, index), piece(owner, index), act_send.at[kind, slot], act_recv.at[kind, slot], device
        )
        copy.start()
        act_copies.append(copy)
        return copy

    stage_y, stage_x, stage_xy, stage_core = [], [], [], []
    arrivals = [(0, None)] + lev_copies
    for slot, (shift, copy) in enumerate(arrivals):
        owner = lax.rem(z + 4 - shift, 4)
        if copy is not None:
            copy.wait_recv()
        stage_y.append(share(owner, mine, shift, 0, (beside, col)))
        stage_x.append(share(owner, mine, shift, 1, (me, across)))
        stage_core.append(share(owner, mine, shift, 3, (me, core)))
    for slot, (shift, _) in enumerate(arrivals):
        owner = lax.rem(z + 4 - shift, 4)
        stage_y[slot].wait_recv()
        stage_xy.append(share(owner, other_mine, shift, 2, (me, across)))
        stage_core.append(share(owner, other_mine, shift, 4, (me, core)))
        stage_x[slot].wait_recv()
        stage_core.append(share(owner, mine_across, shift, 5, (me, core)))
    cast_chunk(1)
    for slot, (shift, _) in enumerate(arrivals):
        owner = lax.rem(z + 4 - shift, 4)
        stage_xy[slot].wait_recv()
        stage_core.append(share(owner, other_across, shift, 6, (me, core)))
    for copy in stage_core:
        copy.wait_recv()

    def part_copy(u, to_peer):
        return send(
            partial.at[u],
            (crossing if to_peer else partial).at[u],
            part_send.at[u],
            (cross_recv if to_peer else part_recv).at[u],
            (inward, col),
        )

    def hid_copy(u):
        return send(hidden.at[u], hidden.at[u], hid_send.at[u], hid_recv.at[u], (outward, col))

    their_rows = row_block(1 - y, rows)

    def grad_cols(k):
        return pl.ds(pl.multiple_of(y * half + k * width, width), width)

    def grad_copy(k):
        return send(
            grad_buf.at[k, :, their_rows],
            grads.at[:, :, grad_cols(k)],
            grad_send.at[k],
            grad_recv.at[k],
            (beside, col),
        )

    def grad_store(k):
        return pltpu.make_async_copy(
            grad_buf.at[k, :, my_rows], grads.at[:, :, grad_cols(k)], store_sem.at[k]
        )

    def multiply(u):
        k, g = lax.div(u, groups), lax.rem(u, groups)

        @pl.when(g == 0)
        def _():
            @pl.when(k + 2 < chunks)
            def _():
                cast_chunk(k + 2)

            weight_copy(k).wait_recv()

        spot = row_block(g, group)
        sums = [
            jnp.dot(left[a, spot], weights[k, a], preferred_element_type=jnp.float32) for a in range(2)
        ]

        @pl.when(outer)
        def _():
            for a in range(2):
                partial[u, a] = sums[a].astype(jnp.bfloat16)
            part_copy(u, False).start()

        @pl.when(inner)
        def _():
            part_copy(u, False).wait_recv()
            for a in range(2):
                partial[u, a] = (partial[u, a].astype(jnp.float32) + sums[a]).astype(jnp.bfloat16)
            part_copy(u, True).start()

        @pl.when(k == 0)
        def _():
            for a in range(2):
                left_t[a, :, spot] = left[a, spot].T

    def activate(u):
        part_copy(u, True).wait_recv()
        pre_act, act_grad = [
            partial[u, a].astype(jnp.float32) + crossing[u, a].astype(jnp.float32) for a in range(2)
        ]
        scale = 0.7978845608028654
        square = pre_act * pre_act
        bent = jnp.tanh(scale * (pre_act + 0.044715 * (square * pre_act)))
        lift = 0.5 * (1.0 + bent)
        slope = lift + 0.5 * pre_act * (1.0 - bent * bent) * (scale * (1.0 + 3 * 0.044715 * square))
        hidden[u, 0] = (act_grad * slope).astype(jnp.bfloat16)
        hidden[u, 1] = (pre_act * lift).astype(jnp.bfloat16)
        hid_copy(u).start()

    def finish_chunk(k):
        for a in range(2):
            total = jnp.zeros((1, width), jnp.float32)
            for block in range(2):
                span = pl.ds(block * rows, rows)
                grad = jnp.zeros((rows, width), jnp.float32)
                for g in range(groups):
                    grad += jnp.dot(
                        left_t[a, span, pl.ds(g * group, group)],
                        hidden[k * groups + g, a],
                        preferred_element_type=jnp.float32,
                    )
                grad_buf[k, a, span] = grad.astype(jnp.bfloat16)
                squares = grad * grad + tiny_value
                total += jnp.sum(squares, axis=0, keepdims=True)
                lanes = squares[:, :128]
                for at in range(128, width, 128):
                    lanes += squares[:, at : at + 128]
                row_acc[a, span] += lanes
            col_parts[z, a : a + 1, pl.ds(pl.multiple_of(k * width, width), width)] = total
        grad_copy(k).start()
        grad_store(k).start()

    behind = jnp.where(inner, 1, lag)

    @pl.loop(0, units + lag)
    def _(s):
        @pl.when(s < units)
        def _():
            multiply(s)

        v = s - behind

        @pl.when(jnp.logical_and(v >= 0, v < units))
        def _():
            @pl.when(inner)
            def _():
                activate(v)

            @pl.when(outer)
            def _():
                hid_copy(v).wait_recv()

            @pl.when(lax.rem(v, groups) == groups - 1)
            def _():
                finish_chunk(lax.div(v, groups))

    col_copies = []
    for shift in range(1, 4):
        to = lax.rem(z + shift, 4)
        copy = send(
            col_parts.at[z], col_parts.at[z], col_send.at[shift - 1], col_recv.at[shift - 1], (to * 2 + y, col)
        )
        copy.start()
        col_copies.append(copy)
    for copy in col_copies:
        copy.wait_recv()
    col_total = col_parts[0] + col_parts[1] + col_parts[2] + col_parts[3]
    for a, old in enumerate((col_up, col_down)):
        kept = old[:, pl.ds(pl.multiple_of(y * half, half), half)]
        fresh = decay_rate * kept + (1.0 - decay_rate) * col_total[a : a + 1] / depth
        col_halves[y, a : a + 1] = fresh
        inverse[a : a + 1] = 1.0 / fresh
    half_copy = send(col_halves.at[y], col_halves.at[y], half_send, half_recv, (beside, col))
    half_copy.start()

    @pl.loop(0, chunks)
    def _(k):
        for a in range(2):
            for block in range(2):
                span = pl.ds(block * rows, rows)
                grad = grad_buf[k, a, span].astype(jnp.float32)
                weighed = grad * grad * inverse[a : a + 1, pl.ds(pl.multiple_of(k * width, width), width)]
                lanes = weighed[:, :128]
                for at in range(128, width, 128):
                    lanes += weighed[:, at : at + 128]
                spent_acc[a, span] += lanes

    for place_at, source in ((0, row_acc), (2, spent_acc)):
        for a in range(2):
            line = jnp.sum(source[a].T, axis=0, keepdims=True)
            for owner in range(2):
                stats[owner, place_at + a : place_at + a + 1] = line[:, owner * rows : (owner + 1) * rows]
    stat_buf[mine] = stats[y]
    stat_copies = []
    for shift in range(1, 8):
        to = level[shift - 1]
        copy = send(
            stats.at[lax.div(to, 4)],
            stat_buf.at[mine],
            stat_send.at[shift - 1],
            stat_recv.at[shift - 1],
            level_device(to),
        )
        copy.start()
        stat_copies.append(copy)
    for copy in stat_copies:
        copy.wait_recv()
    total = stat_buf[0]
    for source in range(1, 8):
        total = total + stat_buf[source]
    for a, old in enumerate((row_up, row_down)):
        fresh = decay_rate * old[...] + (1.0 - decay_rate) * total[a : a + 1] / breadth
        row_new[a : a + 1] = fresh
        spent = jnp.sum(total[2 + a : 3 + a] / fresh, axis=1, keepdims=True)
        energy_buf[me, a : a + 1] = jnp.broadcast_to(spent, (1, 128))
    energy_copies = []
    for shift, other in enumerate(peers):
        copy = send(
            energy_buf.at[me], energy_buf.at[me], energy_send.at[shift], energy_recv.at[shift], (other, col)
        )
        copy.start()
        energy_copies.append(copy)
    half_copy.wait_recv()
    for owner in range(2):
        col_new[:, owner * half : (owner + 1) * half] = col_halves[owner]
    for copy in energy_copies:
        copy.wait_recv()
    summed = energy_buf[0]
    for source in range(1, 8):
        summed = summed + energy_buf[source]
    energy[...] = summed

    for copy in [copy for _, copy in lev_copies] + act_copies + col_copies:
        copy.wait_send()
    for copy in [half_copy] + stat_copies + energy_copies:
        copy.wait_send()

    @pl.loop(0, chunks)
    def _(k):
        weight_copy(k).wait_send()
        grad_copy(k).wait_send()
        grad_copy(k).wait_recv()
        grad_store(k).wait()

    @pl.loop(0, units)
    def _(u):
        part_copy(u, False).wait_send()

        @pl.when(inner)
        def _():
            hid_copy(u).wait_send()


def block_step(pool, visible, out_grad, ln_gain, master_up, master_down, row_up, col_up, row_down, col_down):
    rows, cols = master_up.shape
    tokens, depth = out_grad.shape
    half = cols // 2
    width = 256 if half % 256 == 0 else 128
    chunks = half // width
    groups = 4
    lag = 8
    units = chunks * groups
    deep, part = 2 * rows, tokens // 4
    group = 8 * part
    f32, bf16 = jnp.float32, jnp.bfloat16
    anywhere = pl.BlockSpec(memory_space=pl.ANY)
    vmem = pl.BlockSpec(memory_space=pltpu.VMEM)
    sem = pltpu.SemaphoreType.DMA
    grads, row_new, col_new, energy = pl.pallas_call(
        functools.partial(block_step_kernel, (chunks, width, groups, lag)),
        out_shape=(
            jax.ShapeDtypeStruct((2, rows, cols), bf16),
            jax.ShapeDtypeStruct((2, rows), f32),
            jax.ShapeDtypeStruct((2, cols), f32),
            jax.ShapeDtypeStruct((2, 128), f32),
        ),
        in_specs=[anywhere, vmem, anywhere, vmem, anywhere, anywhere, vmem, vmem, vmem, vmem],
        out_specs=(anywhere, vmem, vmem, vmem),
        scratch_shapes=[
            pltpu.VMEM(pool.shape, bf16),
            pltpu.VMEM(out_grad.shape, f32),
            pltpu.VMEM((2, part, depth), bf16),
            pltpu.VMEM((2, groups * group, deep), bf16),
            pltpu.VMEM((2, deep, groups * group), bf16),
            pltpu.VMEM((chunks, 2, 2, rows, width), f32),
            pltpu.VMEM((chunks, 2, rows, width), bf16),
            pltpu.VMEM((chunks, 2, deep, width), bf16),
            pltpu.VMEM((units, 2, group, width), bf16),
            pltpu.VMEM((units, 2, group, width), bf16),
            pltpu.VMEM((units, 2, group, width), bf16),
            pltpu.VMEM((chunks, 2, deep, width), bf16),
            pltpu.VMEM((4, 2, half), f32),
            pltpu.VMEM((2, 2, half), f32),
            pltpu.VMEM((2, half), f32),
            pltpu.VMEM((2, deep, 128), f32),
            pltpu.VMEM((2, deep, 128), f32),
            pltpu.VMEM((2, 4, rows), f32),
            pltpu.VMEM((8, 4, rows), f32),
            pltpu.VMEM((8, 2, 128), f32),
            sem((2,)),
            sem((chunks, 4)),
            sem((3,)),
            sem((3,)),
            sem((7, 4)),
            sem((7, 4)),
            sem((chunks,)),
            sem((chunks,)),
            sem((units,)),
            sem((units,)),
            sem((units,)),
            sem((units,)),
            sem((units,)),
            sem((chunks,)),
            sem((chunks,)),
            sem((chunks,)),
            sem((3,)),
            sem((3,)),
            sem,
            sem,
            sem((7,)),
            sem((7,)),
            sem((7,)),
            sem((7,)),
        ],
        compiler_params=pltpu.CompilerParams(
            collective_id=0, has_side_effects=True, vmem_limit_bytes=60 * 1024 * 1024
        ),
        name="block_step",
    )(
        pool,
        visible.reshape(1, -1),
        out_grad,
        ln_gain.reshape(1, -1),
        master_up,
        master_down,
        row_up.reshape(1, -1),
        row_down.reshape(1, -1),
        col_up.reshape(1, -1),
        col_down.reshape(1, -1),
    )
    shrink = jnp.maximum(1.0, jnp.sqrt(energy[:, 0] / (depth * cols * 4)))
    updates = [
        finish_update(grads[a].astype(f32), row_new[a], col_new[a]) / shrink[a] for a in range(2)
    ]
    return (updates[0], updates[1], row_new[0], col_new[0], row_new[1], col_new[1])


def suits_block_step(pool, out_grad, master):
    rows, cols = master.shape
    tokens, depth = out_grad.shape
    return (
        lax.axis_size("dp") == 8
        and lax.axis_size("mp") == 4
        and rows * 8 == depth
        and rows % 64 == 0
        and cols % 256 == 0
        and cols >= 512
        and tokens % 64 == 0
        and pool.shape[0] % 16 == 0
    )


def on_device(
    token_pool,
    visible,
    out_grad,
    ln_gain,
    master_up,
    master_down,
    row_up,
    col_up,
    row_down,
    col_down,
):
    if suits_block_step(token_pool, out_grad, master_up):
        return block_step(
            token_pool,
            visible,
            out_grad,
            ln_gain,
            master_up,
            master_down,
            row_up,
            col_up,
            row_down,
            col_down,
        )
    picked = jnp.take(token_pool, visible, axis=0).astype(jnp.float32)
    normed = normalize(picked, ln_gain)
    grid_rows = master_up.shape[0]
    grid_cols = master_up.shape[1]
    depth = grid_rows * lax.axis_size("dp")
    breadth = grid_cols * lax.axis_size("mp")
    w_up = master_up.astype(jnp.bfloat16)
    w_down = master_down.astype(jnp.bfloat16)
    grad_up, grad_down = gathered_grads(normed, out_grad, w_up, w_down)
    squares_up = grad_up * grad_up + tiny_value
    squares_down = grad_down * grad_down + tiny_value
    rowpart_up = jnp.sum(squares_up, axis=1)
    rowpart_down = jnp.sum(squares_down, axis=1)
    colpart_up = jnp.sum(squares_up, axis=0)
    colpart_down = jnp.sum(squares_down, axis=0)
    rowsum_up, rowsum_down = lax.psum((rowpart_up, rowpart_down), "mp")
    colsum_up, colsum_down = lax.psum((colpart_up, colpart_down), "dp")
    row_up_new = decay_rate * row_up + (1.0 - decay_rate) * rowsum_up / breadth
    row_down_new = decay_rate * row_down + (1.0 - decay_rate) * rowsum_down / breadth
    col_up_new = decay_rate * col_up + (1.0 - decay_rate) * colsum_up / depth
    col_down_new = decay_rate * col_down + (1.0 - decay_rate) * colsum_down / depth
    raw_up = finish_update(grad_up, row_up_new, col_up_new)
    raw_down = finish_update(grad_down, row_down_new, col_down_new)
    energy_up, energy_down = lax.psum(
        (jnp.sum(raw_up * raw_up), jnp.sum(raw_down * raw_down)), ("dp", "mp")
    )
    update_up = raw_up / jnp.maximum(1.0, jnp.sqrt(energy_up / (depth * breadth)))
    update_down = raw_down / jnp.maximum(1.0, jnp.sqrt(energy_down / (depth * breadth)))
    return (update_up, update_down, row_up_new, col_up_new, row_down_new, col_down_new)


def solution(mesh):
    return jax.shard_map(
        on_device,
        mesh=mesh,
        in_specs=(
            P("dp", None),
            P("dp"),
            P("dp", None),
            P(),
            P("dp", "mp"),
            P("dp", "mp"),
            P("dp"),
            P("mp"),
            P("dp"),
            P("mp"),
        ),
        out_specs=(P("dp", "mp"), P("dp", "mp"), P("dp"), P("mp"), P("dp"), P("mp")),
        check_vma=False,
    )
```

```python
import functools
import jax
import jax.numpy as jnp
from jax import lax
from jax.experimental import pallas as pl
from jax.experimental.pallas import tpu as pltpu
from jax.sharding import PartitionSpec as P

decay_rate = 0.8
norm_eps = 1e-06
tiny_value = 1e-30


def gelu_tanh(values):
    return jax.nn.gelu(values, approximate=True)


def normalize(values, gain):
    mean_val = jnp.mean(values, axis=1, keepdims=True)
    centred = values - mean_val
    variance = jnp.mean(centred * centred, axis=1, keepdims=True)
    return (centred * lax.rsqrt(variance + norm_eps) * gain).astype(jnp.bfloat16)


def contract_tokens(left, right):
    return lax.dot_general(
        left, right, (((0,), (0,)), ((), ())), preferred_element_type=jnp.float32
    )


def finish_update(grad, row_new, col_new):
    return grad * lax.rsqrt(row_new[:, None] * col_new[None, :])


def gathered_grads(normed, out_grad, w_up, w_down):
    left = normed
    pre_act = jnp.dot(
        left, lax.all_gather(w_up, "dp", axis=0, tiled=True), preferred_element_type=jnp.float32
    )
    act_value, pull_back = jax.vjp(gelu_tanh, pre_act)
    hidden_act = act_value.astype(jnp.bfloat16)
    left = out_grad
    act_grad = jnp.dot(
        left, lax.all_gather(w_down, "dp", axis=0, tiled=True), preferred_element_type=jnp.float32
    )
    pre_grad = pull_back(act_grad)[0].astype(jnp.bfloat16)
    grad_down = lax.psum_scatter(
        contract_tokens(out_grad, hidden_act), "dp", scatter_dimension=0, tiled=True
    )
    grad_up = lax.psum_scatter(
        contract_tokens(normed, pre_grad), "dp", scatter_dimension=0, tiled=True
    )
    return grad_up, grad_down


MESH = pl.DeviceIdType.MESH


def flipped(index):
    return index + 1 - 2 * lax.rem(index, 2)


def greet(devices):
    barrier = pltpu.get_barrier_semaphore()
    for device in devices:
        pl.semaphore_signal(barrier, inc=1, device_id=device, device_id_type=MESH)
    pl.semaphore_wait(barrier, len(devices))


def send(src, dst, send_sem, recv_sem, device):
    return pltpu.make_async_remote_copy(
        src_ref=src,
        dst_ref=dst,
        send_sem=send_sem,
        recv_sem=recv_sem,
        device_id=device,
        device_id_type=MESH,
    )


def block_step_kernel(
    sizes,
    pool,
    visible,
    out_grad,
    gain,
    master_up,
    master_down,
    row_up,
    row_down,
    col_up,
    col_down,
    grads,
    row_new,
    col_new,
    energy,
    pool_buf,
    picked,
    means,
    scales,
    acts,
    left,
    left_t,
    masters,
    cast_out,
    weights,
    partial,
    crossing,
    hidden,
    grad_buf,
    col_parts,
    col_halves,
    row_buf,
    col_buf,
    sum_buf,
    row_acc,
    spent_acc,
    stats,
    stat_buf,
    energy_buf,
    local_sem,
    master_sem,
    lev_send,
    lev_recv,
    act_send,
    act_recv,
    weight_send,
    weight_recv,
    part_send,
    part_recv,
    cross_recv,
    hid_send,
    hid_recv,
    grad_send,
    grad_recv,
    store_sem,
    col_send,
    col_recv,
    half_send,
    half_recv,
    stat_send,
    stat_recv,
    energy_send,
    energy_recv,
    out_sem,
):
    chunks, width, span, first_chunks, lag_inner, lag_outer = sizes
    me = lax.axis_index("dp")
    col = lax.axis_index("mp")
    z = lax.div(me, 2)
    y = lax.rem(me, 2)
    inner = jnp.logical_or(z == 1, z == 2)
    outer = jnp.logical_not(inner)
    rows = master_up.shape[0]
    half = master_up.shape[1] // 2
    depth = rows * 8
    breadth = master_up.shape[1] * 4
    deep = 2 * rows
    block = out_grad.shape[0]
    part = block // 4
    group = span * block
    groups = 8 // span
    units = chunks * groups
    slots = part_send.shape[0]
    mine = y * 4 + col
    beside = flipped(me)
    core = flipped(col)
    across = lax.rem(col + 2, 4)
    near = jnp.where(z < 2, 1, 2)
    inward = me + jnp.where(z < 2, 2, -2)
    outward = me - jnp.where(z < 2, 2, -2)
    masters_in = (master_up, master_down)
    peers = [lax.rem(me + shift, 8) for shift in range(1, 8)]
    level = [lax.rem(mine + shift, 8) for shift in range(1, 8)]
    barrier = pltpu.get_barrier_semaphore()
    greeted = (
        [(other, col) for other in peers]
        + [(me, lax.rem(col + shift, 4)) for shift in range(1, 4)]
        + [(beside, lax.rem(col + shift, 4)) for shift in range(1, 4)]
    )
    for device in greeted:
        pl.semaphore_signal(barrier, inc=1, device_id=device, device_id_type=MESH)

    def place(owner):
        return jnp.where(owner == 0, 2, jnp.where(owner == 1, 0, jnp.where(owner == 2, 1, 3)))

    def level_device(index):
        return (z * 2 + lax.div(index, 4), lax.rem(index, 4))

    def cut(index, size):
        return pl.ds(pl.multiple_of(index * size, size), size)

    load_pool = pltpu.make_async_copy(pool, pool_buf, local_sem.at[0])
    load_out = pltpu.make_async_copy(out_grad.at[cut(col, part)], acts.at[1], local_sem.at[1])

    load_mine = pltpu.make_async_copy(
        out_grad.at[:, cut(z, deep)], left.at[1, cut(place(z), block)], local_sem.at[2]
    )

    def master_loads(late):
        copies = []
        for a in range(2):
            for side in range(2):
                owner = y if side == 0 else 1 - y
                start = pl.multiple_of(owner * half + late * first_chunks * width, width)
                cols = pl.ds(start, half - first_chunks * width if late else first_chunks * width)
                copies.append(
                    pltpu.make_async_copy(
                        masters_in[a].at[:, cols], masters.at[a, :, cols], master_sem.at[late, 2 * a + side]
                    )
                )
        return copies

    load_pool.start()
    load_out.start()
    load_mine.start()
    for copy in master_loads(0):
        copy.start()

    my_rows = cut(y, rows)
    their_rows = cut(1 - y, rows)

    def weight_copy(k):
        return send(
            cast_out.at[k],
            weights.at[k, :, my_rows],
            weight_send.at[lax.rem(k, 6)],
            weight_recv.at[lax.rem(k, 6)],
            (beside, col),
        )

    def strip(owner, k):
        return pl.ds(pl.multiple_of(owner * half + k * width, width), width)

    def cast_theirs(k):
        for a in range(2):
            cast_out[k, a] = masters[a, :, strip(1 - y, k)].astype(jnp.bfloat16)
        weight_copy(k).start()

    def cast_mine(k):
        for a in range(2):
            weights[k, a, my_rows] = masters[a, :, strip(y, k)].astype(jnp.bfloat16)

    load_pool.wait()
    for copy in master_loads(1):
        copy.start()
    places = lax.broadcasted_iota(jnp.int32, (pool.shape[0], block), 0)
    chosen = (places == visible[...]).astype(jnp.bfloat16)
    for level_at in range(4):
        at = pl.ds(level_at * deep, deep)
        picked[:, at] = contract_tokens(chosen, pool_buf[:, at])
    values = picked[...]
    mean_val = jnp.mean(values, axis=1, keepdims=True)
    centred = values - mean_val
    variance = jnp.mean(centred * centred, axis=1, keepdims=True)
    means[...] = mean_val
    scales[...] = lax.rsqrt(variance + norm_eps)

    def normed_at(some, at):
        shifted = picked[some, at] - means[some]
        return (shifted * scales[some] * gain[:, at]).astype(jnp.bfloat16)

    acts[0] = normed_at(cut(col, part), pl.ds(0, depth))
    left[0, cut(place(z), block)] = normed_at(pl.ds(0, block), cut(z, deep))
    load_out.wait()
    load_mine.wait()
    pl.semaphore_wait(barrier, len(greeted))

    first = jnp.where(inner, 3 - z, near)
    second = jnp.where(inner, jnp.where(z == 1, 0, 3), 3 - near)
    third = jnp.where(z < 2, 3, 0)
    owners = [z, first, second, third]
    spots = [place(owner) for owner in owners]

    def piece(spot, quarter):
        return left.at[:, pl.ds(pl.multiple_of(spot * block + quarter * part, part), part)]

    def lev_copy(to, source):
        return send(
            acts.at[:, :, cut(to, deep)],
            piece(place(source), col),
            lev_send.at[to],
            lev_recv.at[source],
            (to * 2 + y, col),
        )

    def lev_start():
        for to in owners[1:]:
            lev_copy(to, z).start()

    def share(kind, at, src, dst, quarter, device):
        return send(
            piece(src, quarter), piece(dst, quarter), act_send.at[kind, at], act_recv.at[kind, at], device
        )

    def along_x(at):
        return share(0, at, at, at, col, (me, across))

    def along_y(at):
        return share(1, at, at, 4 + at, col, (beside, col))

    def turned(at):
        return share(2, at, 4 + at, 4 + at, col, (me, across))

    def to_core(at, far, quarter):
        spot = at + 4 * far
        return share(3 + 2 * far + quarter, at, spot, spot, across if quarter else col, (me, core))

    def spread_out(at):
        along_x(at).start()
        along_y(at).start()
        to_core(at, 0, 0).start()

    def crossed_x(at):
        along_x(at).wait_recv()
        to_core(at, 0, 1).start()

    def crossed_y(index):
        at = spots[index]
        along_y(at).wait_recv()
        turned(at).start()
        to_core(at, 1, 0).start()

    def crossed_both(index):
        turned(spots[index]).wait_recv()
        to_core(spots[index], 1, 1).start()

    def ready(spot):
        for quarter in range(2):
            to_core(spot % 4, spot // 4, quarter).wait_recv()

    def arrive(index):
        lev_copy(owners[index], owners[index]).wait_recv()
        spread_out(spots[index])

    along_y(spots[0]).start()

    @pl.when(inner)
    def _():
        lev_start()

    for copy in master_loads(0):
        copy.wait()
    cast_theirs(0)
    for k in range(first_chunks):
        cast_mine(k)
    row_acc[...] = jnp.zeros_like(row_acc)
    spent_acc[...] = jnp.zeros_like(spent_acc)
    lev_copy(first, first).wait_recv()

    @pl.when(outer)
    def _():
        lev_start()

    spread_out(spots[1])
    cast_theirs(1)
    for copy in master_loads(1):
        copy.wait()

    def run(steps):
        for step, index in steps:
            step(index)

    def cross_x(index):
        crossed_x(spots[index])

    outer_steps = {
        0: [(crossed_y, 0), (arrive, 2), (cross_x, 1), (cross_x, 2)],
        1: [(arrive, 3), (crossed_both, 0)],
    }
    inner_steps = {
        0: [(crossed_y, 0), (cross_x, 1), (arrive, 2), (arrive, 3), (crossed_both, 0), (cross_x, 2)],
        1: [],
    }
    if first_chunks == 2:
        both = {
            2: [(cross_x, 3), (crossed_y, 1)],
            3: [(crossed_y, 2), (crossed_y, 3), (crossed_both, 1)],
            4: [(crossed_both, 2)],
            5: [(crossed_both, 3)],
        }
    else:
        both = {
            3: [(cross_x, 3)],
            4: [(crossed_y, 1)],
            5: [(crossed_y, 2), (crossed_y, 3), (crossed_both, 1)],
            6: [(crossed_both, 2)],
            7: [(crossed_both, 3)],
        }

    @pl.when(outer)
    def _():
        run(outer_steps[0])

    @pl.when(inner)
    def _():
        run(inner_steps[0])

    for k in range(2, first_chunks):
        cast_theirs(k)

    def part_copy(u, slot, to_peer):
        return send(
            partial.at[u],
            (crossing if to_peer else partial).at[u],
            part_send.at[slot],
            (cross_recv if to_peer else part_recv).at[slot],
            (inward, col),
        )

    def hid_copy(u, slot):
        return send(hidden.at[u], hidden.at[u], hid_send.at[slot], hid_recv.at[slot], (outward, col))

    def grad_cols(k):
        return pl.ds(pl.multiple_of(y * half + k * width, width), width)

    def grad_copy(k):
        return send(
            grad_buf.at[k, :, their_rows],
            grads.at[:, :, grad_cols(k)],
            grad_send.at[k],
            grad_recv.at[k],
            (beside, col),
        )

    def grad_store(k):
        return pltpu.make_async_copy(
            grad_buf.at[k, :, my_rows], grads.at[:, :, grad_cols(k)], store_sem.at[k]
        )

    def col_copies(k):
        copies = []
        for shift in range(1, 4):
            copies.append(
                send(
                    col_parts.at[z, k],
                    col_parts.at[z, k],
                    col_send.at[shift - 1, lax.rem(k, 8)],
                    col_recv.at[shift - 1, lax.rem(k, 8)],
                    (lax.rem(z + shift, 4) * 2 + y, col),
                )
            )
        return copies

    def unit(step):
        early = step < first_chunks * groups
        k = jnp.where(early, lax.rem(step, first_chunks), lax.div(step, groups))
        g = jnp.where(early, lax.div(step, first_chunks), lax.rem(step, groups))
        return k, g, k * groups + g, lax.rem(step, slots)

    def multiply(step):
        k, g, u, slot = unit(step)

        @pl.when(step >= slots)
        def _():
            part_copy(u, slot, False).wait_send()

        @pl.when(jnp.logical_and(g == 2, jnp.logical_and(k + 2 >= first_chunks, k + 2 < chunks)))
        def _():
            @pl.when(k >= 4)
            def _():
                weight_copy(k - 4).wait_send()

            cast_theirs(k + 2)
            cast_mine(k + 2)

        @pl.when(g == 0)
        def _():
            weight_copy(k).wait_recv()

        spot = cut(g, group)
        sums = [
            jnp.dot(left[a, spot], weights[k, a], preferred_element_type=jnp.float32) for a in range(2)
        ]

        @pl.when(outer)
        def _():
            for a in range(2):
                partial[u, a] = sums[a].astype(jnp.bfloat16)
            part_copy(u, slot, False).start()

        @pl.when(inner)
        def _():
            part_copy(u, slot, False).wait_recv()
            for a in range(2):
                partial[u, a] = (partial[u, a].astype(jnp.float32) + sums[a]).astype(jnp.bfloat16)
            part_copy(u, slot, True).start()

        @pl.when(k == 0)
        def _():
            for a in range(2):
                left_t[a, :, spot] = left[a, spot].T

    def activate(u, slot):
        part_copy(u, slot, True).wait_recv()
        pre_act, act_grad = [
            partial[u, a].astype(jnp.float32) + crossing[u, a].astype(jnp.float32) for a in range(2)
        ]
        scale = 0.7978845608028654
        square = pre_act * pre_act
        bent = jnp.tanh(scale * (pre_act + 0.044715 * (square * pre_act)))
        lift = 0.5 * (1.0 + bent)
        slope = lift + 0.5 * pre_act * (1.0 - bent * bent) * (scale * (1.0 + 3 * 0.044715 * square))
        hidden[u, 0] = (act_grad * slope).astype(jnp.bfloat16)
        hidden[u, 1] = (pre_act * lift).astype(jnp.bfloat16)
        hid_copy(u, slot).start()

    def fold(values):
        lanes = values[:, :128]
        for at in range(128, width, 128):
            lanes += values[:, at : at + 128]
        return lanes

    def finish_cols(k):
        for copy in col_copies(k):
            copy.wait_recv()
        total = col_parts[0, k] + col_parts[1, k] + col_parts[2, k] + col_parts[3, k]
        at = pl.multiple_of(k * width, width)
        for a, old in enumerate((col_up, col_down)):
            kept = old[:, pl.ds(pl.multiple_of(y * half + at, width), width)]
            fresh = decay_rate * kept + (1.0 - decay_rate) * total[a : a + 1] / depth
            col_halves[y, a : a + 1, pl.ds(at, width)] = fresh
            inverse = 1.0 / fresh
            for side in range(2):
                strip = pl.ds(side * rows, rows)
                grad = grad_buf[k, a, strip].astype(jnp.float32)
                spent_acc[a, strip] += fold(grad * grad * inverse)

    def finish_chunk(k):
        for a in range(2):
            total = jnp.zeros((1, width), jnp.float32)
            for side in range(2):
                strip = pl.ds(side * rows, rows)
                grad = jnp.zeros((rows, width), jnp.float32)
                for g in range(groups):
                    grad += jnp.dot(
                        left_t[a, strip, pl.ds(g * group, group)],
                        hidden[k * groups + g, a],
                        preferred_element_type=jnp.float32,
                    )
                grad_buf[k, a, strip] = grad.astype(jnp.bfloat16)
                squares = grad * grad + tiny_value
                total += jnp.sum(squares, axis=0, keepdims=True)
                row_acc[a, strip] += fold(squares)
            col_parts[z, k, a : a + 1] = total
        @pl.when(k >= 8)
        def _():
            for copy in col_copies(k):
                copy.wait_send()

        for copy in col_copies(k):
            copy.start()
        grad_copy(k).start()
        grad_store(k).start()

        @pl.when(k > 2)
        def _():
            finish_cols(k - 3)

    behind = jnp.where(inner, lag_inner, lag_outer)

    @pl.loop(0, units + lag_outer)
    def _(s):
        @pl.when(jnp.logical_and(s == 1, outer))
        def _():
            run(outer_steps[1])

        for at in both:
            @pl.when(s == at)
            def _():
                run(both[at])

        for g in range(groups):
            @pl.when(s == g * first_chunks)
            def _():
                for spot in range(g * span, (g + 1) * span):
                    if spot < 4:
                        @pl.when(spots[0] != spot)
                        def _():
                            ready(spot)
                    else:
                        ready(spot)

        @pl.when(s < units)
        def _():
            multiply(s)

        v = s - behind

        @pl.when(jnp.logical_and(v >= 0, v < units))
        def _():
            k, g, u, slot = unit(v)

            @pl.when(jnp.logical_and(inner, v >= slots))
            def _():
                hid_copy(u, slot).wait_send()

            @pl.when(inner)
            def _():
                activate(u, slot)

            @pl.when(outer)
            def _():
                hid_copy(u, slot).wait_recv()

            @pl.when(g == groups - 1)
            def _():
                finish_chunk(k)

    def put_lines(place_at, source):
        for a in range(2):
            line = jnp.sum(source[a].T, axis=0, keepdims=True)
            for owner in range(2):
                stats[owner, place_at + a : place_at + a + 1] = line[:, owner * rows : (owner + 1) * rows]

    put_lines(0, row_acc)
    for k in range(chunks - 3, chunks):
        finish_cols(k)
    put_lines(2, spent_acc)
    stat_buf[mine] = stats[y]
    stat_copies = []
    for shift in range(1, 8):
        to = level[shift - 1]
        copy = send(
            stats.at[lax.div(to, 4)],
            stat_buf.at[mine],
            stat_send.at[shift - 1],
            stat_recv.at[shift - 1],
            level_device(to),
        )
        copy.start()
        stat_copies.append(copy)
    half_copy = send(col_halves.at[y], col_halves.at[y], half_send, half_recv, (beside, col))
    half_copy.start()
    for copy in stat_copies:
        copy.wait_recv()
    total = stat_buf[0]
    for source in range(1, 8):
        total = total + stat_buf[source]
    for a, old in enumerate((row_up, row_down)):
        fresh = decay_rate * old[...].reshape(1, rows) + (1.0 - decay_rate) * total[a : a + 1] / breadth
        row_buf[a : a + 1] = fresh
        spent = jnp.sum(total[2 + a : 3 + a] / fresh, axis=1, keepdims=True)
        energy_buf[me, a : a + 1] = jnp.broadcast_to(spent, (1, 128))
    energy_copies = []
    for shift, other in enumerate(peers):
        copy = send(
            energy_buf.at[me], energy_buf.at[me], energy_send.at[shift], energy_recv.at[shift], (other, col)
        )
        copy.start()
        energy_copies.append(copy)
    row_out = pltpu.make_async_copy(row_buf, row_new, out_sem.at[0])
    row_out.start()
    half_copy.wait_recv()
    for owner in range(2):
        col_buf[0:2, owner * half : (owner + 1) * half] = col_halves[owner]
    col_out = pltpu.make_async_copy(col_buf, col_new, out_sem.at[1])
    col_out.start()

    for shift in range(1, 4):
        lev_copy(lax.rem(z + shift, 4), z).wait_send()
    for at in range(4):
        for copy in [along_y(at), turned(at), to_core(at, 1, 0), to_core(at, 1, 1)]:
            copy.wait_send()

        @pl.when(spots[0] != at)
        def _():
            for copy in [along_x(at), to_core(at, 0, 0), to_core(at, 0, 1)]:
                copy.wait_send()

    @pl.loop(0, slots)
    def _(slot):
        part_copy(slot, slot, False).wait_send()

        @pl.when(inner)
        def _():
            hid_copy(slot, slot).wait_send()

    @pl.loop(0, chunks)
    def _(k):
        grad_copy(k).wait_send()
        grad_copy(k).wait_recv()
        grad_store(k).wait()

        @pl.when(k >= chunks - 8)
        def _():
            for copy in col_copies(k):
                copy.wait_send()

        @pl.when(k >= chunks - 6)
        def _():
            weight_copy(k).wait_send()

    for copy in energy_copies:
        copy.wait_recv()
    summed = energy_buf[0]
    for source in range(1, 8):
        summed = summed + energy_buf[source]
    sum_buf[0:2] = summed
    sum_out = pltpu.make_async_copy(sum_buf, energy, out_sem.at[2])
    sum_out.start()
    row_out.wait()
    col_out.wait()
    sum_out.wait()
    for copy in [half_copy] + stat_copies + energy_copies:
        copy.wait_send()


def scale_kernel(count, grads, row_new, col_new, energy, *outs):
    updates, row_outs, col_outs = outs[:2], outs[2:4], outs[4:6]
    upright = outs[6]
    size = grads.shape[1]
    at = pl.program_id(0)

    @pl.when(at == 0)
    def _():
        shrink = jnp.maximum(1.0, jnp.sqrt(energy[...] / count))
        upright[...] = (lax.rsqrt(row_new[...]) / shrink[:, 0:1]).T
        for a in range(2):
            row_outs[a][...] = row_new[a, :]
            col_outs[a][...] = col_new[a, :]

    cols = lax.rsqrt(col_new[...])
    tall = upright[pl.ds(pl.multiple_of(at * size, size), size), :]
    for a in range(2):
        updates[a][...] = grads[a].astype(jnp.float32) * tall[:, a : a + 1] * cols[a : a + 1]


def finish_all(grads, row_new, col_new, energy, count):
    rows, cols = grads.shape[1:]
    size = 64
    f32 = jnp.float32
    tall = pl.BlockSpec((size, cols), lambda i: (i, 0))
    update = jax.ShapeDtypeStruct((rows, cols), f32)
    outs = pl.pallas_call(
        functools.partial(scale_kernel, count),
        grid=(rows // size,),
        out_shape=(
            update,
            update,
            jax.ShapeDtypeStruct((rows,), f32),
            jax.ShapeDtypeStruct((rows,), f32),
            jax.ShapeDtypeStruct((cols,), f32),
            jax.ShapeDtypeStruct((cols,), f32),
        ),
        in_specs=[
            pl.BlockSpec((2, size, cols), lambda i: (0, i, 0)),
            pl.BlockSpec((8, rows), lambda i: (0, 0)),
            pl.BlockSpec((8, cols), lambda i: (0, 0)),
            pl.BlockSpec((8, 128), lambda i: (0, 0)),
        ],
        out_specs=(
            tall,
            tall,
            pl.BlockSpec((rows,), lambda i: (0,)),
            pl.BlockSpec((rows,), lambda i: (0,)),
            pl.BlockSpec((cols,), lambda i: (0,)),
            pl.BlockSpec((cols,), lambda i: (0,)),
        ),
        scratch_shapes=[pltpu.VMEM((rows, 8), f32)],
        compiler_params=pltpu.CompilerParams(vmem_limit_bytes=60 * 1024 * 1024),
        cost_estimate=pl.CostEstimate(
            flops=4 * rows * cols, bytes_accessed=12 * rows * cols, transcendentals=0
        ),
        name="scale",
    )(grads, row_new, col_new, energy)
    return (outs[0], outs[1], outs[2], outs[4], outs[3], outs[5])


def block_step(pool, visible, out_grad, ln_gain, master_up, master_down, row_up, col_up, row_down, col_down):
    rows, cols = master_up.shape
    tokens, depth = out_grad.shape
    half = cols // 2
    width = 128
    span = 2
    chunks = half // width
    groups = 8 // span
    units = chunks * groups
    deep, part = 2 * rows, tokens // 4
    group = span * tokens
    f32, bf16 = jnp.float32, jnp.bfloat16
    anywhere = pl.BlockSpec(memory_space=pl.ANY)
    vmem = pl.BlockSpec(memory_space=pltpu.VMEM)
    sem = pltpu.SemaphoreType.DMA
    grads, row_new, col_new, energy = pl.pallas_call(
        functools.partial(block_step_kernel, (chunks, width, span, 2, 2, 8)),
        out_shape=(
            jax.ShapeDtypeStruct((2, rows, cols), bf16),
            jax.ShapeDtypeStruct((8, rows), f32),
            jax.ShapeDtypeStruct((8, cols), f32),
            jax.ShapeDtypeStruct((8, 128), f32),
        ),
        in_specs=[anywhere, vmem, anywhere, vmem, anywhere, anywhere, vmem, vmem, vmem, vmem],
        out_specs=(anywhere,) * 4,
        scratch_shapes=[
            pltpu.VMEM(pool.shape, bf16),
            pltpu.VMEM(out_grad.shape, f32),
            pltpu.VMEM((tokens, 1), f32),
            pltpu.VMEM((tokens, 1), f32),
            pltpu.VMEM((2, part, depth), bf16),
            pltpu.VMEM((2, groups * group, deep), bf16),
            pltpu.VMEM((2, deep, groups * group), bf16),
            pltpu.VMEM((2, rows, cols), f32),
            pltpu.VMEM((chunks, 2, rows, width), bf16),
            pltpu.VMEM((chunks, 2, deep, width), bf16),
            pltpu.VMEM((units, 2, group, width), bf16),
            pltpu.VMEM((units, 2, group, width), bf16),
            pltpu.VMEM((units, 2, group, width), bf16),
            pltpu.VMEM((chunks, 2, deep, width), bf16),
            pltpu.VMEM((4, chunks, 2, width), f32),
            pltpu.VMEM((2, 2, half), f32),
            pltpu.VMEM((8, rows), f32),
            pltpu.VMEM((8, cols), f32),
            pltpu.VMEM((8, 128), f32),
            pltpu.VMEM((2, deep, 128), f32),
            pltpu.VMEM((2, deep, 128), f32),
            pltpu.VMEM((2, 4, rows), f32),
            pltpu.VMEM((8, 4, rows), f32),
            pltpu.VMEM((8, 2, 128), f32),
            sem((3,)),
            sem((2, 4)),
            sem((4,)),
            sem((4,)),
            sem((7, 4)),
            sem((7, 4)),
            sem((6,)),
            sem((6,)),
            sem((12,)),
            sem((12,)),
            sem((12,)),
            sem((12,)),
            sem((12,)),
            sem((chunks,)),
            sem((chunks,)),
            sem((chunks,)),
            sem((3, 8)),
            sem((3, 8)),
            sem,
            sem,
            sem((7,)),
            sem((7,)),
            sem((7,)),
            sem((7,)),
            sem((3,)),
        ],
        compiler_params=pltpu.CompilerParams(
            collective_id=0, has_side_effects=True, vmem_limit_bytes=60 * 1024 * 1024
        ),
        name="block_step",
    )(
        pool,
        visible.reshape(1, -1),
        out_grad,
        ln_gain.reshape(1, -1),
        master_up,
        master_down,
        row_up,
        row_down,
        col_up.reshape(1, -1),
        col_down.reshape(1, -1),
    )
    return finish_all(grads, row_new, col_new, energy, depth * cols * 4)


def suits_block_step(pool, out_grad, master):
    rows, cols = master.shape
    tokens, depth = out_grad.shape
    return (
        lax.axis_size("dp") == 8
        and lax.axis_size("mp") == 4
        and rows * 8 == depth
        and rows % 64 == 0
        and cols % 256 == 0
        and cols >= 512
        and tokens % 64 == 0
        and pool.shape[0] % 16 == 0
    )


def on_device(
    token_pool,
    visible,
    out_grad,
    ln_gain,
    master_up,
    master_down,
    row_up,
    col_up,
    row_down,
    col_down,
):
    if suits_block_step(token_pool, out_grad, master_up):
        return block_step(
            token_pool,
            visible,
            out_grad,
            ln_gain,
            master_up,
            master_down,
            row_up,
            col_up,
            row_down,
            col_down,
        )
    picked = jnp.take(token_pool, visible, axis=0).astype(jnp.float32)
    normed = normalize(picked, ln_gain)
    grid_rows = master_up.shape[0]
    grid_cols = master_up.shape[1]
    depth = grid_rows * lax.axis_size("dp")
    breadth = grid_cols * lax.axis_size("mp")
    w_up = master_up.astype(jnp.bfloat16)
    w_down = master_down.astype(jnp.bfloat16)
    grad_up, grad_down = gathered_grads(normed, out_grad, w_up, w_down)
    squares_up = grad_up * grad_up + tiny_value
    squares_down = grad_down * grad_down + tiny_value
    rowpart_up = jnp.sum(squares_up, axis=1)
    rowpart_down = jnp.sum(squares_down, axis=1)
    colpart_up = jnp.sum(squares_up, axis=0)
    colpart_down = jnp.sum(squares_down, axis=0)
    rowsum_up, rowsum_down = lax.psum((rowpart_up, rowpart_down), "mp")
    colsum_up, colsum_down = lax.psum((colpart_up, colpart_down), "dp")
    row_up_new = decay_rate * row_up + (1.0 - decay_rate) * rowsum_up / breadth
    row_down_new = decay_rate * row_down + (1.0 - decay_rate) * rowsum_down / breadth
    col_up_new = decay_rate * col_up + (1.0 - decay_rate) * colsum_up / depth
    col_down_new = decay_rate * col_down + (1.0 - decay_rate) * colsum_down / depth
    raw_up = finish_update(grad_up, row_up_new, col_up_new)
    raw_down = finish_update(grad_down, row_down_new, col_down_new)
    energy_up, energy_down = lax.psum(
        (jnp.sum(raw_up * raw_up), jnp.sum(raw_down * raw_down)), ("dp", "mp")
    )
    update_up = raw_up / jnp.maximum(1.0, jnp.sqrt(energy_up / (depth * breadth)))
    update_down = raw_down / jnp.maximum(1.0, jnp.sqrt(energy_down / (depth * breadth)))
    return (update_up, update_down, row_up_new, col_up_new, row_down_new, col_down_new)


def solution(mesh):
    return jax.shard_map(
        on_device,
        mesh=mesh,
        in_specs=(
            P("dp", None),
            P("dp"),
            P("dp", None),
            P(),
            P("dp", "mp"),
            P("dp", "mp"),
            P("dp"),
            P("mp"),
            P("dp"),
            P("mp"),
        ),
        out_specs=(P("dp", "mp"), P("dp", "mp"), P("dp"), P("mp"), P("dp"), P("mp")),
        check_vma=False,
    )
```

```python
import functools
import jax
import jax.numpy as jnp
from jax import lax
from jax.experimental import pallas as pl
from jax.experimental.pallas import tpu as pltpu
from jax.sharding import PartitionSpec as P

decay_rate = 0.8
norm_eps = 1e-06
tiny_value = 1e-30


def gelu_tanh(values):
    return jax.nn.gelu(values, approximate=True)


def normalize(values, gain):
    mean_val = jnp.mean(values, axis=1, keepdims=True)
    centred = values - mean_val
    variance = jnp.mean(centred * centred, axis=1, keepdims=True)
    return (centred * lax.rsqrt(variance + norm_eps) * gain).astype(jnp.bfloat16)


def contract_tokens(left, right):
    return lax.dot_general(
        left, right, (((0,), (0,)), ((), ())), preferred_element_type=jnp.float32
    )


def finish_update(grad, row_new, col_new):
    return grad * lax.rsqrt(row_new[:, None] * col_new[None, :])


def gathered_grads(normed, out_grad, w_up, w_down):
    left = normed
    pre_act = jnp.dot(
        left, lax.all_gather(w_up, "dp", axis=0, tiled=True), preferred_element_type=jnp.float32
    )
    act_value, pull_back = jax.vjp(gelu_tanh, pre_act)
    hidden_act = act_value.astype(jnp.bfloat16)
    left = out_grad
    act_grad = jnp.dot(
        left, lax.all_gather(w_down, "dp", axis=0, tiled=True), preferred_element_type=jnp.float32
    )
    pre_grad = pull_back(act_grad)[0].astype(jnp.bfloat16)
    grad_down = lax.psum_scatter(
        contract_tokens(out_grad, hidden_act), "dp", scatter_dimension=0, tiled=True
    )
    grad_up = lax.psum_scatter(
        contract_tokens(normed, pre_grad), "dp", scatter_dimension=0, tiled=True
    )
    return grad_up, grad_down


MESH = pl.DeviceIdType.MESH


def flipped(index):
    return index + 1 - 2 * lax.rem(index, 2)


def greet(devices):
    barrier = pltpu.get_barrier_semaphore()
    for device in devices:
        pl.semaphore_signal(barrier, inc=1, device_id=device, device_id_type=MESH)
    pl.semaphore_wait(barrier, len(devices))


def send(src, dst, send_sem, recv_sem, device):
    return pltpu.make_async_remote_copy(
        src_ref=src,
        dst_ref=dst,
        send_sem=send_sem,
        recv_sem=recv_sem,
        device_id=device,
        device_id_type=MESH,
    )


def block_step_kernel(
    sizes,
    pool,
    visible,
    out_grad,
    gain,
    master_up,
    master_down,
    row_up,
    row_down,
    col_up,
    col_down,
    grads,
    row_new,
    col_new,
    energy,
    pool_buf,
    picked,
    means,
    scales,
    acts,
    left,
    left_t,
    masters,
    cast_out,
    weights,
    partial,
    crossing,
    hidden,
    grad_buf,
    col_parts,
    col_halves,
    row_buf,
    col_buf,
    sum_buf,
    row_acc,
    spent_acc,
    stats,
    stat_buf,
    energy_buf,
    local_sem,
    master_sem,
    lev_send,
    lev_recv,
    act_send,
    act_recv,
    weight_send,
    weight_recv,
    part_send,
    part_recv,
    cross_recv,
    hid_send,
    hid_recv,
    grad_send,
    grad_recv,
    store_sem,
    col_send,
    col_recv,
    half_send,
    half_recv,
    stat_send,
    stat_recv,
    energy_send,
    energy_recv,
    out_sem,
):
    chunks, width, span, first_chunks, lag_inner, lag_outer = sizes
    me = lax.axis_index("dp")
    col = lax.axis_index("mp")
    z = lax.div(me, 2)
    y = lax.rem(me, 2)
    inner = jnp.logical_or(z == 1, z == 2)
    outer = jnp.logical_not(inner)
    rows = master_up.shape[0]
    half = master_up.shape[1] // 2
    depth = rows * 8
    breadth = master_up.shape[1] * 4
    deep = 2 * rows
    block = out_grad.shape[0]
    part = block // 4
    group = span * block
    groups = 8 // span
    units = chunks * groups
    mine = y * 4 + col
    beside = flipped(me)
    core = flipped(col)
    across = lax.rem(col + 2, 4)
    near = jnp.where(z < 2, 1, 2)
    inward = me + jnp.where(z < 2, 2, -2)
    outward = me - jnp.where(z < 2, 2, -2)
    masters_in = (master_up, master_down)
    peers = [lax.rem(me + shift, 8) for shift in range(1, 8)]
    level = [lax.rem(mine + shift, 8) for shift in range(1, 8)]
    barrier = pltpu.get_barrier_semaphore()
    greeted = (
        [(other, col) for other in peers]
        + [(me, lax.rem(col + shift, 4)) for shift in range(1, 4)]
        + [(beside, lax.rem(col + shift, 4)) for shift in range(1, 4)]
    )
    for device in greeted:
        pl.semaphore_signal(barrier, inc=1, device_id=device, device_id_type=MESH)

    def place(owner):
        return jnp.where(owner == 0, 2, jnp.where(owner == 1, 0, jnp.where(owner == 2, 1, 3)))

    def level_device(index):
        return (z * 2 + lax.div(index, 4), lax.rem(index, 4))

    def cut(index, size):
        return pl.ds(pl.multiple_of(index * size, size), size)

    pool_loads = []
    for at in range(4):
        cols = pl.ds(at * deep, deep)
        pool_loads.append(pltpu.make_async_copy(pool.at[:, cols], pool_buf.at[:, cols], local_sem.at[2 + at]))
    load_out = pltpu.make_async_copy(out_grad.at[cut(col, part)], acts.at[1], local_sem.at[1])

    load_mine = pltpu.make_async_copy(
        out_grad.at[:, cut(z, deep)], left.at[1, cut(place(z), block)], local_sem.at[0]
    )

    def master_loads(late):
        copies = []
        for a in range(2):
            for side in range(2):
                owner = y if side == 0 else 1 - y
                start = pl.multiple_of(owner * half + late * first_chunks * width, width)
                cols = pl.ds(start, half - first_chunks * width if late else first_chunks * width)
                copies.append(
                    pltpu.make_async_copy(
                        masters_in[a].at[:, cols], masters.at[a, :, cols], master_sem.at[late, 2 * a + side]
                    )
                )
        return copies

    for load in pool_loads:
        load.start()
    load_out.start()
    load_mine.start()

    my_rows = cut(y, rows)
    their_rows = cut(1 - y, rows)

    def weight_copy(k):
        return send(
            cast_out.at[k],
            weights.at[k, :, my_rows],
            weight_send.at[lax.rem(k, 6)],
            weight_recv.at[lax.rem(k, 6)],
            (beside, col),
        )

    def strip(owner, k):
        return pl.ds(pl.multiple_of(owner * half + k * width, width), width)

    def cast_theirs(k):
        for a in range(2):
            cast_out[k, a] = masters[a, :, strip(1 - y, k)].astype(jnp.bfloat16)
        weight_copy(k).start()

    def cast_mine(k):
        for a in range(2):
            weights[k, a, my_rows] = masters[a, :, strip(y, k)].astype(jnp.bfloat16)

    places = lax.broadcasted_iota(jnp.int32, (pool.shape[0], block), 0)
    chosen = (places == visible[...]).astype(jnp.bfloat16)
    for level_at, load in enumerate(pool_loads):
        load.wait()
        at = pl.ds(level_at * deep, deep)
        picked[:, at] = contract_tokens(chosen, pool_buf[:, at])
        if level_at == 1:
            for copy in master_loads(0):
                copy.start()
    values = picked[...]
    mean_val = jnp.mean(values, axis=1, keepdims=True)
    centred = values - mean_val
    variance = jnp.mean(centred * centred, axis=1, keepdims=True)
    means[...] = mean_val
    scales[...] = lax.rsqrt(variance + norm_eps)

    def normed_at(some, at):
        shifted = picked[some, at] - means[some]
        return (shifted * scales[some] * gain[:, at]).astype(jnp.bfloat16)

    acts[0] = normed_at(cut(col, part), pl.ds(0, depth))
    left[0, cut(place(z), block)] = normed_at(pl.ds(0, block), cut(z, deep))
    load_out.wait()
    load_mine.wait()
    pl.semaphore_wait(barrier, len(greeted))

    first = jnp.where(inner, 3 - z, near)
    second = jnp.where(inner, jnp.where(z == 1, 0, 3), 3 - near)
    third = jnp.where(z < 2, 3, 0)
    owners = [z, first, second, third]
    spots = [place(owner) for owner in owners]

    def piece(spot, quarter):
        return left.at[:, pl.ds(pl.multiple_of(spot * block + quarter * part, part), part)]

    def lev_copy(to, source):
        return send(
            acts.at[:, :, cut(to, deep)],
            piece(place(source), col),
            lev_send.at[to],
            lev_recv.at[source],
            (to * 2 + y, col),
        )

    def lev_start():
        for to in owners[1:]:
            lev_copy(to, z).start()

    def share(kind, at, src, dst, quarter, device):
        return send(
            piece(src, quarter), piece(dst, quarter), act_send.at[kind, at], act_recv.at[kind, at], device
        )

    def along_x(at):
        return share(0, at, at, at, col, (me, across))

    def along_y(at):
        return share(1, at, at, 4 + at, col, (beside, col))

    def turned(at):
        return share(2, at, 4 + at, 4 + at, col, (me, across))

    def to_core(at, far, quarter):
        spot = at + 4 * far
        return share(3 + 2 * far + quarter, at, spot, spot, across if quarter else col, (me, core))

    def spread_out(at):
        along_x(at).start()
        along_y(at).start()
        to_core(at, 0, 0).start()

    def crossed_x(at):
        along_x(at).wait_recv()
        to_core(at, 0, 1).start()

    def crossed_y(index):
        at = spots[index]
        along_y(at).wait_recv()
        turned(at).start()
        to_core(at, 1, 0).start()

    def crossed_both(index):
        turned(spots[index]).wait_recv()
        to_core(spots[index], 1, 1).start()

    def ready(spot):
        for quarter in range(2):
            to_core(spot % 4, spot // 4, quarter).wait_recv()

    def arrive(index):
        lev_copy(owners[index], owners[index]).wait_recv()
        spread_out(spots[index])

    along_y(spots[0]).start()

    @pl.when(inner)
    def _():
        lev_start()

    for copy in master_loads(0):
        copy.wait()
    cast_theirs(0)
    for k in range(first_chunks):
        cast_mine(k)
    row_acc[...] = jnp.zeros_like(row_acc)
    spent_acc[...] = jnp.zeros_like(spent_acc)
    lev_copy(first, first).wait_recv()

    @pl.when(outer)
    def _():
        lev_start()

    spread_out(spots[1])
    for k in range(1, first_chunks):
        cast_theirs(k)
    for copy in master_loads(1):
        copy.start()

    def run(steps):
        for step, index in steps:
            step(index)

    def cross_x(index):
        crossed_x(spots[index])

    outer_steps = {
        0: [(crossed_y, 0), (arrive, 2), (cross_x, 1), (cross_x, 2)],
        1: [(arrive, 3), (crossed_both, 0)],
    }
    inner_steps = {
        0: [(crossed_y, 0), (cross_x, 1), (arrive, 2), (arrive, 3), (crossed_both, 0), (cross_x, 2)],
        1: [],
    }
    both = {
        2: [(cross_x, 3), (crossed_y, 1)],
        3: [(crossed_y, 2), (crossed_y, 3), (crossed_both, 1)],
        4: [(crossed_both, 2)],
        5: [(crossed_both, 3)],
    }

    @pl.when(outer)
    def _():
        run(outer_steps[0])

    @pl.when(inner)
    def _():
        run(inner_steps[0])

    def part_copy(u, step, to_peer):
        recv = cross_recv if to_peer else part_recv
        return send(
            partial.at[u],
            (crossing if to_peer else partial).at[u],
            part_send.at[lax.rem(step, 8)],
            recv.at[lax.rem(step, recv.shape[0])],
            (inward, col),
        )

    def hid_copy(u, step):
        return send(
            hidden.at[u],
            hidden.at[u],
            hid_send.at[lax.rem(step, 8)],
            hid_recv.at[lax.rem(step, hid_recv.shape[0])],
            (outward, col),
        )

    def grad_cols(k):
        return pl.ds(pl.multiple_of(y * half + k * width, width), width)

    def grad_copy(k):
        return send(
            grad_buf.at[k, :, their_rows],
            grads.at[:, :, grad_cols(k)],
            grad_send.at[lax.rem(k, 2)],
            grad_recv.at[k],
            (beside, col),
        )

    def grad_store(k):
        return pltpu.make_async_copy(
            grad_buf.at[k, :, my_rows], grads.at[:, :, grad_cols(k)], store_sem.at[lax.rem(k, 2)]
        )

    def col_copies(k):
        copies = []
        for shift in range(1, 4):
            copies.append(
                send(
                    col_parts.at[z, k],
                    col_parts.at[z, k],
                    col_send.at[shift - 1, lax.rem(k, 2)],
                    col_recv.at[shift - 1, lax.rem(k, 8)],
                    (lax.rem(z + shift, 4) * 2 + y, col),
                )
            )
        return copies

    def unit(step):
        early = step < first_chunks * groups
        k = jnp.where(early, lax.rem(step, first_chunks), lax.div(step, groups))
        g = jnp.where(early, lax.div(step, first_chunks), lax.rem(step, groups))
        return k, g, k * groups + g

    def multiply(step):
        k, g, u = unit(step)

        @pl.when(step >= 8)
        def _():
            part_copy(u, step, False).wait_send()

        @pl.when(jnp.logical_and(g == groups // 2, jnp.logical_and(k + 2 >= first_chunks, k + 2 < chunks)))
        def _():
            @pl.when(k >= 4)
            def _():
                weight_copy(k - 4).wait_send()

            cast_theirs(k + 2)
            cast_mine(k + 2)

        @pl.when(g == 0)
        def _():
            weight_copy(k).wait_recv()

        spot = cut(g, group)
        sums = [
            jnp.dot(left[a, spot], weights[k, a], preferred_element_type=jnp.float32) for a in range(2)
        ]

        @pl.when(outer)
        def _():
            for a in range(2):
                partial[u, a] = sums[a].astype(jnp.bfloat16)
            part_copy(u, step, False).start()

        @pl.when(inner)
        def _():
            part_copy(u, step, False).wait_recv()
            for a in range(2):
                partial[u, a] = (partial[u, a].astype(jnp.float32) + sums[a]).astype(jnp.bfloat16)
            part_copy(u, step, True).start()

        @pl.when(k == 0)
        def _():
            for a in range(2):
                left_t[a, :, spot] = left[a, spot].T

    def activate(u, step):
        part_copy(u, step, True).wait_recv()
        pre_act, act_grad = [
            partial[u, a].astype(jnp.float32) + crossing[u, a].astype(jnp.float32) for a in range(2)
        ]
        scale = 0.7978845608028654
        square = pre_act * pre_act
        bent = jnp.tanh(scale * (pre_act + 0.044715 * (square * pre_act)))
        lift = 0.5 * (1.0 + bent)
        slope = lift + 0.5 * pre_act * (1.0 - bent * bent) * (scale * (1.0 + 3 * 0.044715 * square))
        hidden[u, 0] = (act_grad * slope).astype(jnp.bfloat16)
        hidden[u, 1] = (pre_act * lift).astype(jnp.bfloat16)
        hid_copy(u, step).start()

    def fold(values):
        lanes = values[:, :128]
        for at in range(128, width, 128):
            lanes += values[:, at : at + 128]
        return lanes

    def finish_cols(k):
        for copy in col_copies(k):
            copy.wait_recv()
        total = col_parts[0, k] + col_parts[1, k] + col_parts[2, k] + col_parts[3, k]
        at = pl.multiple_of(k * width, width)
        for a, old in enumerate((col_up, col_down)):
            kept = old[:, pl.ds(pl.multiple_of(y * half + at, width), width)]
            fresh = decay_rate * kept + (1.0 - decay_rate) * total[a : a + 1] / depth
            col_halves[y, a : a + 1, pl.ds(at, width)] = fresh
            inverse = 1.0 / fresh
            for side in range(2):
                strip = pl.ds(side * rows, rows)
                grad = grad_buf[k, a, strip].astype(jnp.float32)
                spent_acc[a, strip] += fold(grad * grad * inverse)

    def finish_chunk(k):
        for a in range(2):
            total = jnp.zeros((1, width), jnp.float32)
            for side in range(2):
                strip = pl.ds(side * rows, rows)
                grad = jnp.zeros((rows, width), jnp.float32)
                for g in range(groups):
                    grad += jnp.dot(
                        left_t[a, strip, pl.ds(g * group, group)],
                        hidden[k * groups + g, a],
                        preferred_element_type=jnp.float32,
                    )
                grad_buf[k, a, strip] = grad.astype(jnp.bfloat16)
                squares = grad * grad + tiny_value
                total += jnp.sum(squares, axis=0, keepdims=True)
                row_acc[a, strip] += fold(squares)
            col_parts[z, k, a : a + 1] = total
        @pl.when(k >= 2)
        def _():
            for copy in col_copies(k):
                copy.wait_send()
            grad_copy(k).wait_send()
            grad_store(k).wait()

        for copy in col_copies(k):
            copy.start()
        grad_copy(k).start()
        grad_store(k).start()

        @pl.when(k > 2)
        def _():
            finish_cols(k - 3)

    behind = jnp.where(inner, lag_inner, lag_outer)

    @pl.loop(0, units + lag_outer)
    def _(s):
        @pl.when(jnp.logical_and(s == 1, outer))
        def _():
            run(outer_steps[1])

        @pl.when(s == 0)
        def _():
            for copy in master_loads(1):
                copy.wait()

        for at in both:
            @pl.when(s == at * 2 // span)
            def _():
                run(both[at])

        for g in range(groups):
            @pl.when(s == g * first_chunks)
            def _():
                for spot in range(g * span, (g + 1) * span):
                    if spot < 4:
                        @pl.when(spots[0] != spot)
                        def _():
                            ready(spot)
                    else:
                        ready(spot)

        @pl.when(s < units)
        def _():
            multiply(s)

        v = s - behind

        @pl.when(jnp.logical_and(v >= 0, v < units))
        def _():
            k, g, u = unit(v)

            @pl.when(jnp.logical_and(inner, v >= 8))
            def _():
                hid_copy(u, v).wait_send()

            @pl.when(inner)
            def _():
                activate(u, v)

            @pl.when(outer)
            def _():
                hid_copy(u, v).wait_recv()

            @pl.when(g == groups - 1)
            def _():
                finish_chunk(k)

    def put_lines(place_at, source):
        for a in range(2):
            line = jnp.sum(source[a].T, axis=0, keepdims=True)
            for owner in range(2):
                stats[owner, place_at + a : place_at + a + 1] = line[:, owner * rows : (owner + 1) * rows]

    put_lines(0, row_acc)
    for k in range(chunks - 3, chunks):
        finish_cols(k)
    put_lines(2, spent_acc)
    stat_buf[mine] = stats[y]
    stat_copies = []
    for shift in range(1, 8):
        to = level[shift - 1]
        copy = send(
            stats.at[lax.div(to, 4)],
            stat_buf.at[mine],
            stat_send.at[shift - 1],
            stat_recv.at[shift - 1],
            level_device(to),
        )
        copy.start()
        stat_copies.append(copy)
    half_copy = send(col_halves.at[y], col_halves.at[y], half_send, half_recv, (beside, col))
    half_copy.start()
    for copy in stat_copies:
        copy.wait_recv()
    total = stat_buf[0]
    for source in range(1, 8):
        total = total + stat_buf[source]
    for a, old in enumerate((row_up, row_down)):
        fresh = decay_rate * old[...].reshape(1, rows) + (1.0 - decay_rate) * total[a : a + 1] / breadth
        row_buf[a : a + 1] = fresh
        spent = jnp.sum(total[2 + a : 3 + a] / fresh, axis=1, keepdims=True)
        energy_buf[me, a : a + 1] = jnp.broadcast_to(spent, (1, 128))
    energy_copies = []
    for shift, other in enumerate(peers):
        copy = send(
            energy_buf.at[me], energy_buf.at[me], energy_send.at[shift], energy_recv.at[shift], (other, col)
        )
        copy.start()
        energy_copies.append(copy)
    row_out = pltpu.make_async_copy(row_buf, row_new, out_sem.at[0])
    row_out.start()
    half_copy.wait_recv()
    for owner in range(2):
        col_buf[0:2, owner * half : (owner + 1) * half] = col_halves[owner]
    col_out = pltpu.make_async_copy(col_buf, col_new, out_sem.at[1])
    col_out.start()

    for shift in range(1, 4):
        lev_copy(lax.rem(z + shift, 4), z).wait_send()
    for at in range(4):
        for copy in [along_y(at), turned(at), to_core(at, 1, 0), to_core(at, 1, 1)]:
            copy.wait_send()

        @pl.when(spots[0] != at)
        def _():
            for copy in [along_x(at), to_core(at, 0, 0), to_core(at, 0, 1)]:
                copy.wait_send()

    @pl.loop(0, 8)
    def _(slot):
        part_copy(slot, slot, False).wait_send()

        @pl.when(inner)
        def _():
            hid_copy(slot, slot).wait_send()

    @pl.loop(0, chunks)
    def _(k):
        grad_copy(k).wait_recv()

        @pl.when(k >= chunks - 2)
        def _():
            grad_copy(k).wait_send()
            grad_store(k).wait()
            for copy in col_copies(k):
                copy.wait_send()

        @pl.when(k >= chunks - 6)
        def _():
            weight_copy(k).wait_send()

    for copy in energy_copies:
        copy.wait_recv()
    summed = energy_buf[0]
    for source in range(1, 8):
        summed = summed + energy_buf[source]
    sum_buf[0:2] = summed
    sum_out = pltpu.make_async_copy(sum_buf, energy, out_sem.at[2])
    sum_out.start()
    row_out.wait()
    col_out.wait()
    sum_out.wait()
    for copy in [half_copy] + stat_copies + energy_copies:
        copy.wait_send()


def scale_kernel(count, grads, row_new, col_new, energy, *outs):
    updates, row_outs, col_outs = outs[:2], outs[2:4], outs[4:6]
    upright = outs[6]
    size = grads.shape[1]
    at = pl.program_id(0)

    @pl.when(at == 0)
    def _():
        shrink = jnp.maximum(1.0, jnp.sqrt(energy[...] / count))
        upright[...] = (lax.rsqrt(row_new[...]) / shrink[:, 0:1]).T
        for a in range(2):
            row_outs[a][...] = row_new[a, :]
            col_outs[a][...] = col_new[a, :]

    cols = lax.rsqrt(col_new[...])
    tall = upright[pl.ds(pl.multiple_of(at * size, size), size), :]
    for a in range(2):
        updates[a][...] = grads[a].astype(jnp.float32) * tall[:, a : a + 1] * cols[a : a + 1]


def finish_all(grads, row_new, col_new, energy, count):
    rows, cols = grads.shape[1:]
    size = 64
    f32 = jnp.float32
    tall = pl.BlockSpec((size, cols), lambda i: (i, 0))
    update = jax.ShapeDtypeStruct((rows, cols), f32)
    outs = pl.pallas_call(
        functools.partial(scale_kernel, count),
        grid=(rows // size,),
        out_shape=(
            update,
            update,
            jax.ShapeDtypeStruct((rows,), f32),
            jax.ShapeDtypeStruct((rows,), f32),
            jax.ShapeDtypeStruct((cols,), f32),
            jax.ShapeDtypeStruct((cols,), f32),
        ),
        in_specs=[
            pl.BlockSpec((2, size, cols), lambda i: (0, i, 0)),
            pl.BlockSpec((8, rows), lambda i: (0, 0)),
            pl.BlockSpec((8, cols), lambda i: (0, 0)),
            pl.BlockSpec((8, 128), lambda i: (0, 0)),
        ],
        out_specs=(
            tall,
            tall,
            pl.BlockSpec((rows,), lambda i: (0,)),
            pl.BlockSpec((rows,), lambda i: (0,)),
            pl.BlockSpec((cols,), lambda i: (0,)),
            pl.BlockSpec((cols,), lambda i: (0,)),
        ),
        scratch_shapes=[pltpu.VMEM((rows, 8), f32)],
        compiler_params=pltpu.CompilerParams(vmem_limit_bytes=24 * 1024 * 1024),
        cost_estimate=pl.CostEstimate(
            flops=4 * rows * cols, bytes_accessed=12 * rows * cols, transcendentals=0
        ),
        name="scale",
    )(grads, row_new, col_new, energy)
    return (outs[0], outs[1], outs[2], outs[4], outs[3], outs[5])


def block_step(pool, visible, out_grad, ln_gain, master_up, master_down, row_up, col_up, row_down, col_down):
    rows, cols = master_up.shape
    tokens, depth = out_grad.shape
    half = cols // 2
    width = 128
    span = 1
    chunks = half // width
    groups = 8 // span
    units = chunks * groups
    deep, part = 2 * rows, tokens // 4
    group = span * tokens
    f32, bf16 = jnp.float32, jnp.bfloat16
    anywhere = pl.BlockSpec(memory_space=pl.ANY)
    vmem = pl.BlockSpec(memory_space=pltpu.VMEM)
    sem = pltpu.SemaphoreType.DMA
    grads, row_new, col_new, energy = pl.pallas_call(
        functools.partial(block_step_kernel, (chunks, width, span, 2, 3, 14)),
        out_shape=(
            pltpu.VMEM((2, rows, cols), bf16),
            pltpu.VMEM((8, rows), f32),
            pltpu.VMEM((8, cols), f32),
            pltpu.VMEM((8, 128), f32),
        ),
        in_specs=[anywhere, vmem, anywhere, vmem, anywhere, anywhere, vmem, vmem, vmem, vmem],
        out_specs=(vmem,) * 4,
        scratch_shapes=[
            pltpu.VMEM(pool.shape, bf16),
            pltpu.VMEM(out_grad.shape, f32),
            pltpu.VMEM((tokens, 1), f32),
            pltpu.VMEM((tokens, 1), f32),
            pltpu.VMEM((2, part, depth), bf16),
            pltpu.VMEM((2, groups * group, deep), bf16),
            pltpu.VMEM((2, deep, groups * group), bf16),
            pltpu.VMEM((2, rows, cols), f32),
            pltpu.VMEM((chunks, 2, rows, width), bf16),
            pltpu.VMEM((chunks, 2, deep, width), bf16),
            pltpu.VMEM((units, 2, group, width), bf16),
            pltpu.VMEM((units, 2, group, width), bf16),
            pltpu.VMEM((units, 2, group, width), bf16),
            pltpu.VMEM((chunks, 2, deep, width), bf16),
            pltpu.VMEM((4, chunks, 2, width), f32),
            pltpu.VMEM((2, 2, half), f32),
            pltpu.VMEM((8, rows), f32),
            pltpu.VMEM((8, cols), f32),
            pltpu.VMEM((8, 128), f32),
            pltpu.VMEM((2, deep, 128), f32),
            pltpu.VMEM((2, deep, 128), f32),
            pltpu.VMEM((2, 4, rows), f32),
            pltpu.VMEM((8, 4, rows), f32),
            pltpu.VMEM((8, 2, 128), f32),
            sem((6,)),
            sem((2, 4)),
            sem((4,)),
            sem((4,)),
            sem((7, 4)),
            sem((7, 4)),
            sem((6,)),
            sem((6,)),
            sem((8,)),
            sem((16,)),
            sem((8,)),
            sem((8,)),
            sem((16,)),
            sem((2,)),
            sem((chunks,)),
            sem((2,)),
            sem((3, 2)),
            sem((3, 8)),
            sem,
            sem,
            sem((7,)),
            sem((7,)),
            sem((7,)),
            sem((7,)),
            sem((3,)),
        ],
        compiler_params=pltpu.CompilerParams(
            collective_id=0, has_side_effects=True, vmem_limit_bytes=56 * 1024 * 1024
        ),
        name="block_step",
    )(
        pool,
        visible.reshape(1, -1),
        out_grad,
        ln_gain.reshape(1, -1),
        master_up,
        master_down,
        row_up,
        row_down,
        col_up.reshape(1, -1),
        col_down.reshape(1, -1),
    )
    return finish_all(grads, row_new, col_new, energy, depth * cols * 4)


def suits_block_step(pool, out_grad, master):
    rows, cols = master.shape
    tokens, depth = out_grad.shape
    return (
        lax.axis_size("dp") == 8
        and lax.axis_size("mp") == 4
        and rows * 8 == depth
        and rows % 64 == 0
        and cols % 256 == 0
        and cols >= 512
        and tokens % 64 == 0
        and pool.shape[0] % 16 == 0
    )


def on_device(
    token_pool,
    visible,
    out_grad,
    ln_gain,
    master_up,
    master_down,
    row_up,
    col_up,
    row_down,
    col_down,
):
    if suits_block_step(token_pool, out_grad, master_up):
        return block_step(
            token_pool,
            visible,
            out_grad,
            ln_gain,
            master_up,
            master_down,
            row_up,
            col_up,
            row_down,
            col_down,
        )
    picked = jnp.take(token_pool, visible, axis=0).astype(jnp.float32)
    normed = normalize(picked, ln_gain)
    grid_rows = master_up.shape[0]
    grid_cols = master_up.shape[1]
    depth = grid_rows * lax.axis_size("dp")
    breadth = grid_cols * lax.axis_size("mp")
    w_up = master_up.astype(jnp.bfloat16)
    w_down = master_down.astype(jnp.bfloat16)
    grad_up, grad_down = gathered_grads(normed, out_grad, w_up, w_down)
    squares_up = grad_up * grad_up + tiny_value
    squares_down = grad_down * grad_down + tiny_value
    rowpart_up = jnp.sum(squares_up, axis=1)
    rowpart_down = jnp.sum(squares_down, axis=1)
    colpart_up = jnp.sum(squares_up, axis=0)
    colpart_down = jnp.sum(squares_down, axis=0)
    rowsum_up, rowsum_down = lax.psum((rowpart_up, rowpart_down), "mp")
    colsum_up, colsum_down = lax.psum((colpart_up, colpart_down), "dp")
    row_up_new = decay_rate * row_up + (1.0 - decay_rate) * rowsum_up / breadth
    row_down_new = decay_rate * row_down + (1.0 - decay_rate) * rowsum_down / breadth
    col_up_new = decay_rate * col_up + (1.0 - decay_rate) * colsum_up / depth
    col_down_new = decay_rate * col_down + (1.0 - decay_rate) * colsum_down / depth
    raw_up = finish_update(grad_up, row_up_new, col_up_new)
    raw_down = finish_update(grad_down, row_down_new, col_down_new)
    energy_up, energy_down = lax.psum(
        (jnp.sum(raw_up * raw_up), jnp.sum(raw_down * raw_down)), ("dp", "mp")
    )
    update_up = raw_up / jnp.maximum(1.0, jnp.sqrt(energy_up / (depth * breadth)))
    update_down = raw_down / jnp.maximum(1.0, jnp.sqrt(energy_down / (depth * breadth)))
    return (update_up, update_down, row_up_new, col_up_new, row_down_new, col_down_new)


def solution(mesh):
    return jax.shard_map(
        on_device,
        mesh=mesh,
        in_specs=(
            P("dp", None),
            P("dp"),
            P("dp", None),
            P(),
            P("dp", "mp"),
            P("dp", "mp"),
            P("dp"),
            P("mp"),
            P("dp"),
            P("mp"),
        ),
        out_specs=(P("dp", "mp"), P("dp", "mp"), P("dp"), P("mp"), P("dp"), P("mp")),
        check_vma=False,
    )
```

```python
import functools
import jax
import jax.numpy as jnp
from jax import lax
from jax.experimental import pallas as pl
from jax.experimental.pallas import tpu as pltpu
from jax.sharding import PartitionSpec as P

decay_rate = 0.8
norm_eps = 1e-06
tiny_value = 1e-30


def gelu_tanh(values):
    return jax.nn.gelu(values, approximate=True)


def normalize(values, gain):
    mean_val = jnp.mean(values, axis=1, keepdims=True)
    centred = values - mean_val
    variance = jnp.mean(centred * centred, axis=1, keepdims=True)
    return (centred * lax.rsqrt(variance + norm_eps) * gain).astype(jnp.bfloat16)


def contract_tokens(left, right):
    return lax.dot_general(
        left, right, (((0,), (0,)), ((), ())), preferred_element_type=jnp.float32
    )


def finish_update(grad, row_new, col_new):
    return grad * lax.rsqrt(row_new[:, None] * col_new[None, :])


def gathered_grads(normed, out_grad, w_up, w_down):
    left = normed
    pre_act = jnp.dot(
        left, lax.all_gather(w_up, "dp", axis=0, tiled=True), preferred_element_type=jnp.float32
    )
    act_value, pull_back = jax.vjp(gelu_tanh, pre_act)
    hidden_act = act_value.astype(jnp.bfloat16)
    left = out_grad
    act_grad = jnp.dot(
        left, lax.all_gather(w_down, "dp", axis=0, tiled=True), preferred_element_type=jnp.float32
    )
    pre_grad = pull_back(act_grad)[0].astype(jnp.bfloat16)
    grad_down = lax.psum_scatter(
        contract_tokens(out_grad, hidden_act), "dp", scatter_dimension=0, tiled=True
    )
    grad_up = lax.psum_scatter(
        contract_tokens(normed, pre_grad), "dp", scatter_dimension=0, tiled=True
    )
    return grad_up, grad_down


MESH = pl.DeviceIdType.MESH


def flipped(index):
    return index + 1 - 2 * lax.rem(index, 2)


def greet(devices):
    barrier = pltpu.get_barrier_semaphore()
    for device in devices:
        pl.semaphore_signal(barrier, inc=1, device_id=device, device_id_type=MESH)
    pl.semaphore_wait(barrier, len(devices))


def send(src, dst, send_sem, recv_sem, device):
    return pltpu.make_async_remote_copy(
        src_ref=src,
        dst_ref=dst,
        send_sem=send_sem,
        recv_sem=recv_sem,
        device_id=device,
        device_id_type=MESH,
    )


def block_step_kernel(
    sizes,
    pool,
    visible,
    out_grad,
    gain,
    master_up,
    master_down,
    row_up,
    row_down,
    col_up,
    col_down,
    grads,
    row_new,
    col_new,
    energy,
    pool_buf,
    picked,
    means,
    scales,
    acts,
    left,
    left_t,
    masters,
    cast_out,
    weights,
    partial,
    crossing,
    hidden,
    grad_buf,
    col_parts,
    col_halves,
    row_buf,
    col_buf,
    sum_buf,
    begun,
    row_acc,
    spent_acc,
    stats,
    stat_buf,
    energy_buf,
    local_sem,
    master_sem,
    lev_send,
    lev_recv,
    act_send,
    act_recv,
    weight_send,
    weight_recv,
    part_send,
    part_recv,
    cross_recv,
    hid_send,
    hid_recv,
    grad_send,
    grad_recv,
    store_sem,
    col_send,
    col_recv,
    half_send,
    half_recv,
    stat_send,
    stat_recv,
    energy_send,
    energy_recv,
    out_sem,
):
    chunks, width, span, first_chunks, lag_inner, lag_outer = sizes
    me = lax.axis_index("dp")
    col = lax.axis_index("mp")
    z = lax.div(me, 2)
    y = lax.rem(me, 2)
    inner = jnp.logical_or(z == 1, z == 2)
    outer = jnp.logical_not(inner)
    rows = master_up.shape[0]
    half = master_up.shape[1] // 2
    depth = rows * 8
    breadth = master_up.shape[1] * 4
    deep = 2 * rows
    block = out_grad.shape[0]
    part = block // 4
    group = span * block
    groups = 8 // span
    units = chunks * groups
    joint = 2 // span
    mine = y * 4 + col
    beside = flipped(me)
    core = flipped(col)
    across = lax.rem(col + 2, 4)
    near = jnp.where(z < 2, 1, 2)
    inward = me + jnp.where(z < 2, 2, -2)
    outward = me - jnp.where(z < 2, 2, -2)
    masters_in = (master_up, master_down)
    peers = [lax.rem(me + shift, 8) for shift in range(1, 8)]
    level = [lax.rem(mine + shift, 8) for shift in range(1, 8)]
    barrier = pltpu.get_barrier_semaphore()
    greeted = (
        [(other, col) for other in peers]
        + [(me, lax.rem(col + shift, 4)) for shift in range(1, 4)]
        + [(beside, lax.rem(col + shift, 4)) for shift in range(1, 4)]
    )
    for device in greeted:
        pl.semaphore_signal(barrier, inc=1, device_id=device, device_id_type=MESH)

    def place(owner):
        return jnp.where(owner == 0, 2, jnp.where(owner == 1, 0, jnp.where(owner == 2, 1, 3)))

    def level_device(index):
        return (z * 2 + lax.div(index, 4), lax.rem(index, 4))

    def cut(index, size):
        return pl.ds(pl.multiple_of(index * size, size), size)

    pool_loads = []
    for at in range(4):
        cols = pl.ds(at * deep, deep)
        pool_loads.append(pltpu.make_async_copy(pool.at[:, cols], pool_buf.at[:, cols], local_sem.at[2 + at]))
    load_out = pltpu.make_async_copy(out_grad.at[cut(col, part)], acts.at[1], local_sem.at[1])

    load_mine = pltpu.make_async_copy(
        out_grad.at[:, cut(z, deep)], left.at[1, cut(place(z), block)], local_sem.at[0]
    )

    def master_loads(late):
        copies = []
        for a in range(2):
            for side in range(2):
                owner = y if side == 0 else 1 - y
                start = pl.multiple_of(owner * half + late * first_chunks * width, width)
                cols = pl.ds(start, half - first_chunks * width if late else first_chunks * width)
                copies.append(
                    pltpu.make_async_copy(
                        masters_in[a].at[:, cols], masters.at[a, :, cols], master_sem.at[late, 2 * a + side]
                    )
                )
        return copies

    for load in pool_loads:
        load.start()
    load_out.start()
    load_mine.start()

    my_rows = cut(y, rows)
    their_rows = cut(1 - y, rows)

    def weight_copy(k):
        return send(
            cast_out.at[k],
            weights.at[k, :, my_rows],
            weight_send.at[lax.rem(k, 6)],
            weight_recv.at[lax.rem(k, 6)],
            (beside, col),
        )

    def strip(owner, k):
        return pl.ds(pl.multiple_of(owner * half + k * width, width), width)

    def cast_theirs(k):
        for a in range(2):
            cast_out[k, a] = masters[a, :, strip(1 - y, k)].astype(jnp.bfloat16)
        weight_copy(k).start()

    def cast_mine(k):
        for a in range(2):
            weights[k, a, my_rows] = masters[a, :, strip(y, k)].astype(jnp.bfloat16)

    places = lax.broadcasted_iota(jnp.int32, (pool.shape[0], block), 0)
    chosen = (places == visible[...]).astype(jnp.bfloat16)
    for level_at, load in enumerate(pool_loads):
        load.wait()
        at = pl.ds(level_at * deep, deep)
        picked[:, at] = contract_tokens(chosen, pool_buf[:, at])
        if level_at == 1:
            for copy in master_loads(0):
                copy.start()
    values = picked[...]
    mean_val = jnp.mean(values, axis=1, keepdims=True)
    centred = values - mean_val
    variance = jnp.mean(centred * centred, axis=1, keepdims=True)
    means[...] = mean_val
    scales[...] = lax.rsqrt(variance + norm_eps)

    def normed_at(some, at):
        shifted = picked[some, at] - means[some]
        return (shifted * scales[some] * gain[:, at]).astype(jnp.bfloat16)

    acts[0] = normed_at(cut(col, part), pl.ds(0, depth))
    left[0, cut(place(z), block)] = normed_at(pl.ds(0, block), cut(z, deep))
    load_out.wait()
    load_mine.wait()
    pl.semaphore_wait(barrier, len(greeted))

    first = jnp.where(inner, 3 - z, near)
    second = jnp.where(inner, jnp.where(z == 1, 0, 3), 3 - near)
    third = jnp.where(z < 2, 3, 0)
    owners = [z, first, second, third]
    spots = [place(owner) for owner in owners]

    def piece(spot, quarter):
        return left.at[:, pl.ds(pl.multiple_of(spot * block + quarter * part, part), part)]

    def lev_copy(to, source):
        return send(
            acts.at[:, :, cut(to, deep)],
            piece(place(source), col),
            lev_send.at[to],
            lev_recv.at[source],
            (to * 2 + y, col),
        )

    def lev_start():
        for to in owners[1:]:
            lev_copy(to, z).start()

    def share(kind, at, src, dst, quarter, device):
        return send(
            piece(src, quarter), piece(dst, quarter), act_send.at[kind, at], act_recv.at[kind, at], device
        )

    def along_x(at):
        return share(0, at, at, at, col, (me, across))

    def along_y(at):
        return share(1, at, at, 4 + at, col, (beside, col))

    def turned(at):
        return share(2, at, 4 + at, 4 + at, col, (me, across))

    def to_core(at, far, quarter):
        spot = at + 4 * far
        return share(3 + 2 * far + quarter, at, spot, spot, across if quarter else col, (me, core))

    def spread_out(at):
        along_x(at).start()
        along_y(at).start()
        to_core(at, 0, 0).start()

    def crossed_x(at):
        along_x(at).wait_recv()
        to_core(at, 0, 1).start()

    def crossed_y(index):
        at = spots[index]
        along_y(at).wait_recv()
        turned(at).start()
        to_core(at, 1, 0).start()

    def crossed_both(index):
        turned(spots[index]).wait_recv()
        to_core(spots[index], 1, 1).start()

    def ready(spot):
        for quarter in range(2):
            to_core(spot % 4, spot // 4, quarter).wait_recv()

    def arrive(index):
        lev_copy(owners[index], owners[index]).wait_recv()
        spread_out(spots[index])

    along_y(spots[0]).start()

    @pl.when(inner)
    def _():
        lev_start()

    for copy in master_loads(0):
        copy.wait()
    for k in range(first_chunks):
        cast_theirs(k)
    for k in range(first_chunks):
        cast_mine(k)
    row_acc[...] = jnp.zeros_like(row_acc)
    spent_acc[...] = jnp.zeros_like(spent_acc)
    lev_copy(first, first).wait_recv()

    @pl.when(outer)
    def _():
        lev_start()

    spread_out(spots[1])
    for copy in master_loads(1):
        copy.start()

    def run(steps):
        for step, index in steps:
            step(index)

    def cross_x(index):
        crossed_x(spots[index])

    outer_steps = {
        0: [(crossed_y, 0), (arrive, 2), (cross_x, 1), (cross_x, 2)],
        1: [(arrive, 3), (crossed_both, 0)],
    }
    inner_steps = {
        0: [(crossed_y, 0), (cross_x, 1), (arrive, 2), (arrive, 3), (crossed_both, 0), (cross_x, 2)],
        1: [],
    }
    both = {
        2: [(cross_x, 3), (crossed_y, 1)],
        3: [(crossed_y, 2), (crossed_y, 3), (crossed_both, 1)],
        4: [(crossed_both, 2)],
        5: [(crossed_both, 3)],
    }

    @pl.when(outer)
    def _():
        run(outer_steps[0])

    @pl.when(inner)
    def _():
        run(inner_steps[0])

    def part_copy(u, step, to_peer):
        recv = cross_recv if to_peer else part_recv
        return send(
            partial.at[u],
            (crossing if to_peer else partial).at[u],
            part_send.at[lax.rem(step, 8)],
            recv.at[lax.rem(step, recv.shape[0])],
            (inward, col),
        )

    def hid_copy(u, step):
        return send(
            hidden.at[u],
            hidden.at[u],
            hid_send.at[lax.rem(step, 8)],
            hid_recv.at[lax.rem(step, hid_recv.shape[0])],
            (outward, col),
        )

    def grad_cols(k):
        return pl.ds(pl.multiple_of(y * half + k * width, width), width)

    def grad_copy(k):
        return send(
            grad_buf.at[k, :, their_rows],
            grads.at[:, :, grad_cols(k)],
            grad_send.at[lax.rem(k, 2)],
            grad_recv.at[k],
            (beside, col),
        )

    def grad_store(k):
        return pltpu.make_async_copy(
            grad_buf.at[k, :, my_rows], grads.at[:, :, grad_cols(k)], store_sem.at[lax.rem(k, 2)]
        )

    def col_copies(k):
        copies = []
        for shift in range(1, 4):
            copies.append(
                send(
                    col_parts.at[z, k],
                    col_parts.at[z, k],
                    col_send.at[shift - 1, lax.rem(k, 2)],
                    col_recv.at[shift - 1, lax.rem(k, 8)],
                    (lax.rem(z + shift, 4) * 2 + y, col),
                )
            )
        return copies

    def unit(step):
        early = step < first_chunks * groups
        pair = lax.div(step, joint)
        k = jnp.where(early, lax.rem(pair, first_chunks), lax.div(step, groups))
        g = jnp.where(
            early,
            lax.div(pair, first_chunks) * joint + lax.rem(step, joint),
            lax.rem(step, groups),
        )
        return k, g, k * groups + g

    def multiply(step):
        k, g, u = unit(step)

        @pl.when(step >= 8)
        def _():
            part_copy(u, step, False).wait_send()

        @pl.when(jnp.logical_and(g == groups // 2, jnp.logical_and(k + 2 >= first_chunks, k + 2 < chunks)))
        def _():
            @pl.when(k >= 4)
            def _():
                weight_copy(k - 4).wait_send()

            cast_theirs(k + 2)
            cast_mine(k + 2)

        @pl.when(g == 0)
        def _():
            weight_copy(k).wait_recv()

        spot = cut(g, group)
        sums = [
            jnp.dot(left[a, spot], weights[k, a], preferred_element_type=jnp.float32) for a in range(2)
        ]

        @pl.when(outer)
        def _():
            for a in range(2):
                partial[u, a] = sums[a].astype(jnp.bfloat16)
            part_copy(u, step, False).start()

        @pl.when(inner)
        def _():
            part_copy(u, step, False).wait_recv()
            for a in range(2):
                partial[u, a] = (partial[u, a].astype(jnp.float32) + sums[a]).astype(jnp.bfloat16)
            part_copy(u, step, True).start()

        @pl.when(k == 0)
        def _():
            for a in range(2):
                left_t[a, :, spot] = left[a, spot].T

    def activate(u, step):
        part_copy(u, step, True).wait_recv()
        pre_act, act_grad = [
            partial[u, a].astype(jnp.float32) + crossing[u, a].astype(jnp.float32) for a in range(2)
        ]
        scale = 0.7978845608028654
        square = pre_act * pre_act
        bent = jnp.tanh(scale * (pre_act + 0.044715 * (square * pre_act)))
        lift = 0.5 * (1.0 + bent)
        slope = lift + 0.5 * pre_act * (1.0 - bent * bent) * (scale * (1.0 + 3 * 0.044715 * square))
        hidden[u, 0] = (act_grad * slope).astype(jnp.bfloat16)
        hidden[u, 1] = (pre_act * lift).astype(jnp.bfloat16)
        hid_copy(u, step).start()

    def fold(values):
        lanes = values[:, :128]
        for at in range(128, width, 128):
            lanes += values[:, at : at + 128]
        return lanes

    def finish_cols(k):
        for copy in col_copies(k):
            copy.wait_recv()
        total = col_parts[0, k] + col_parts[1, k] + col_parts[2, k] + col_parts[3, k]
        at = pl.multiple_of(k * width, width)
        for a, old in enumerate((col_up, col_down)):
            kept = old[:, pl.ds(pl.multiple_of(y * half + at, width), width)]
            fresh = decay_rate * kept + (1.0 - decay_rate) * total[a : a + 1] / depth
            col_halves[y, a : a + 1, pl.ds(at, width)] = fresh
            inverse = 1.0 / fresh
            for side in range(2):
                strip = pl.ds(side * rows, rows)
                grad = grad_buf[k, a, strip].astype(jnp.float32)
                spent_acc[a, strip] += fold(grad * grad * inverse)

    def grad_part(k, a, strip, g):
        return jnp.dot(
            left_t[a, strip, pl.ds(g * group, group)],
            hidden[k * groups + g, a],
            preferred_element_type=jnp.float32,
        )

    def begin_chunk(k):
        for a in range(2):
            for side in range(2):
                strip = pl.ds(side * rows, rows)
                grad = grad_part(k, a, strip, 0)
                for g in range(1, groups - 1):
                    grad += grad_part(k, a, strip, g)
                begun[a, strip] = grad

    def finish_chunk(k):
        for a in range(2):
            total = jnp.zeros((1, width), jnp.float32)
            for side in range(2):
                strip = pl.ds(side * rows, rows)
                grad = begun[a, strip] + grad_part(k, a, strip, groups - 1)
                grad_buf[k, a, strip] = grad.astype(jnp.bfloat16)
                squares = grad * grad + tiny_value
                total += jnp.sum(squares, axis=0, keepdims=True)
                row_acc[a, strip] += fold(squares)
            col_parts[z, k, a : a + 1] = total
        @pl.when(k >= 2)
        def _():
            for copy in col_copies(k):
                copy.wait_send()
            grad_copy(k).wait_send()
            grad_store(k).wait()

        for copy in col_copies(k):
            copy.start()
        grad_copy(k).start()
        grad_store(k).start()

        @pl.when(k > 2)
        def _():
            finish_cols(k - 3)

    behind = jnp.where(inner, lag_inner, lag_outer)

    @pl.loop(0, units + lag_outer)
    def _(s):
        @pl.when(jnp.logical_and(s == 1, outer))
        def _():
            run(outer_steps[1])

        @pl.when(s == 0)
        def _():
            for copy in master_loads(1):
                copy.wait()

        for at in both:
            @pl.when(s == at * 2 // span)
            def _():
                run(both[at])

        for pair in range(4):
            @pl.when(s == pair * joint * first_chunks)
            def _():
                for spot in range(2 * pair, 2 * pair + 2):
                    if spot < 4:
                        @pl.when(spots[0] != spot)
                        def _():
                            ready(spot)
                    else:
                        ready(spot)

        @pl.when(s < units)
        def _():
            multiply(s)

        v = s - behind

        @pl.when(jnp.logical_and(v >= 0, v < units))
        def _():
            k, g, u = unit(v)

            @pl.when(jnp.logical_and(inner, v >= 8))
            def _():
                hid_copy(u, v).wait_send()

            @pl.when(inner)
            def _():
                activate(u, v)

            @pl.when(outer)
            def _():
                hid_copy(u, v).wait_recv()

            @pl.when(g == groups - 2)
            def _():
                begin_chunk(k)

            @pl.when(g == groups - 1)
            def _():
                finish_chunk(k)

    def put_lines(place_at, source):
        for a in range(2):
            line = jnp.sum(source[a].T, axis=0, keepdims=True)
            for owner in range(2):
                stats[owner, place_at + a : place_at + a + 1] = line[:, owner * rows : (owner + 1) * rows]

    put_lines(0, row_acc)
    for k in range(chunks - 3, chunks):
        finish_cols(k)
    put_lines(2, spent_acc)
    stat_buf[mine] = stats[y]
    stat_copies = []
    for shift in range(1, 8):
        to = level[shift - 1]
        copy = send(
            stats.at[lax.div(to, 4)],
            stat_buf.at[mine],
            stat_send.at[shift - 1],
            stat_recv.at[shift - 1],
            level_device(to),
        )
        copy.start()
        stat_copies.append(copy)
    half_copy = send(col_halves.at[y], col_halves.at[y], half_send, half_recv, (beside, col))
    half_copy.start()
    for copy in stat_copies:
        copy.wait_recv()
    total = stat_buf[0]
    for source in range(1, 8):
        total = total + stat_buf[source]
    for a, old in enumerate((row_up, row_down)):
        fresh = decay_rate * old[...].reshape(1, rows) + (1.0 - decay_rate) * total[a : a + 1] / breadth
        row_buf[a : a + 1] = fresh
        spent = jnp.sum(total[2 + a : 3 + a] / fresh, axis=1, keepdims=True)
        energy_buf[me, a : a + 1] = jnp.broadcast_to(spent, (1, 128))
    energy_copies = []
    for shift, other in enumerate(peers):
        copy = send(
            energy_buf.at[me], energy_buf.at[me], energy_send.at[shift], energy_recv.at[shift], (other, col)
        )
        copy.start()
        energy_copies.append(copy)
    row_out = pltpu.make_async_copy(row_buf, row_new, out_sem.at[0])
    row_out.start()
    half_copy.wait_recv()
    for owner in range(2):
        col_buf[0:2, owner * half : (owner + 1) * half] = col_halves[owner]
    col_out = pltpu.make_async_copy(col_buf, col_new, out_sem.at[1])
    col_out.start()

    for shift in range(1, 4):
        lev_copy(lax.rem(z + shift, 4), z).wait_send()
    for at in range(4):
        for copy in [along_y(at), turned(at), to_core(at, 1, 0), to_core(at, 1, 1)]:
            copy.wait_send()

        @pl.when(spots[0] != at)
        def _():
            for copy in [along_x(at), to_core(at, 0, 0), to_core(at, 0, 1)]:
                copy.wait_send()

    @pl.loop(0, 8)
    def _(slot):
        part_copy(slot, slot, False).wait_send()

        @pl.when(inner)
        def _():
            hid_copy(slot, slot).wait_send()

    @pl.loop(0, chunks)
    def _(k):
        grad_copy(k).wait_recv()

        @pl.when(k >= chunks - 2)
        def _():
            grad_copy(k).wait_send()
            grad_store(k).wait()
            for copy in col_copies(k):
                copy.wait_send()

        @pl.when(k >= chunks - 6)
        def _():
            weight_copy(k).wait_send()

    for copy in energy_copies:
        copy.wait_recv()
    summed = energy_buf[0]
    for source in range(1, 8):
        summed = summed + energy_buf[source]
    sum_buf[0:2] = summed
    sum_out = pltpu.make_async_copy(sum_buf, energy, out_sem.at[2])
    sum_out.start()
    row_out.wait()
    col_out.wait()
    sum_out.wait()
    for copy in [half_copy] + stat_copies + energy_copies:
        copy.wait_send()


def scale_kernel(count, grads, row_new, col_new, energy, *outs):
    updates, row_outs, col_outs = outs[:2], outs[2:4], outs[4:6]
    upright = outs[6]
    size = grads.shape[1]
    at = pl.program_id(0)

    @pl.when(at == 0)
    def _():
        shrink = jnp.maximum(1.0, jnp.sqrt(energy[...] / count))
        upright[...] = (lax.rsqrt(row_new[...]) / shrink[:, 0:1]).T
        for a in range(2):
            row_outs[a][...] = row_new[a, :]
            col_outs[a][...] = col_new[a, :]

    cols = lax.rsqrt(col_new[...])
    tall = upright[pl.ds(pl.multiple_of(at * size, size), size), :]
    for a in range(2):
        updates[a][...] = grads[a].astype(jnp.float32) * tall[:, a : a + 1] * cols[a : a + 1]


def finish_all(grads, row_new, col_new, energy, count):
    rows, cols = grads.shape[1:]
    size = 64
    f32 = jnp.float32
    tall = pl.BlockSpec((size, cols), lambda i: (i, 0))
    update = jax.ShapeDtypeStruct((rows, cols), f32)
    outs = pl.pallas_call(
        functools.partial(scale_kernel, count),
        grid=(rows // size,),
        out_shape=(
            update,
            update,
            jax.ShapeDtypeStruct((rows,), f32),
            jax.ShapeDtypeStruct((rows,), f32),
            jax.ShapeDtypeStruct((cols,), f32),
            jax.ShapeDtypeStruct((cols,), f32),
        ),
        in_specs=[
            pl.BlockSpec((2, size, cols), lambda i: (0, i, 0)),
            pl.BlockSpec((8, rows), lambda i: (0, 0)),
            pl.BlockSpec((8, cols), lambda i: (0, 0)),
            pl.BlockSpec((8, 128), lambda i: (0, 0)),
        ],
        out_specs=(
            tall,
            tall,
            pl.BlockSpec((rows,), lambda i: (0,)),
            pl.BlockSpec((rows,), lambda i: (0,)),
            pl.BlockSpec((cols,), lambda i: (0,)),
            pl.BlockSpec((cols,), lambda i: (0,)),
        ),
        scratch_shapes=[pltpu.VMEM((rows, 8), f32)],
        compiler_params=pltpu.CompilerParams(vmem_limit_bytes=24 * 1024 * 1024),
        cost_estimate=pl.CostEstimate(
            flops=4 * rows * cols, bytes_accessed=12 * rows * cols, transcendentals=0
        ),
        name="scale",
    )(grads, row_new, col_new, energy)
    return (outs[0], outs[1], outs[2], outs[4], outs[3], outs[5])


def block_step(pool, visible, out_grad, ln_gain, master_up, master_down, row_up, col_up, row_down, col_down):
    rows, cols = master_up.shape
    tokens, depth = out_grad.shape
    half = cols // 2
    width = 128
    span = 1
    chunks = half // width
    groups = 8 // span
    units = chunks * groups
    deep, part = 2 * rows, tokens // 4
    group = span * tokens
    f32, bf16 = jnp.float32, jnp.bfloat16
    anywhere = pl.BlockSpec(memory_space=pl.ANY)
    vmem = pl.BlockSpec(memory_space=pltpu.VMEM)
    sem = pltpu.SemaphoreType.DMA
    grads, row_new, col_new, energy = pl.pallas_call(
        functools.partial(block_step_kernel, (chunks, width, span, 2, 3, 14)),
        out_shape=(
            pltpu.VMEM((2, rows, cols), bf16),
            pltpu.VMEM((8, rows), f32),
            pltpu.VMEM((8, cols), f32),
            pltpu.VMEM((8, 128), f32),
        ),
        in_specs=[anywhere, vmem, anywhere, vmem, anywhere, anywhere, vmem, vmem, vmem, vmem],
        out_specs=(vmem,) * 4,
        scratch_shapes=[
            pltpu.VMEM(pool.shape, bf16),
            pltpu.VMEM(out_grad.shape, f32),
            pltpu.VMEM((tokens, 1), f32),
            pltpu.VMEM((tokens, 1), f32),
            pltpu.VMEM((2, part, depth), bf16),
            pltpu.VMEM((2, groups * group, deep), bf16),
            pltpu.VMEM((2, deep, groups * group), bf16),
            pltpu.VMEM((2, rows, cols), f32),
            pltpu.VMEM((chunks, 2, rows, width), bf16),
            pltpu.VMEM((chunks, 2, deep, width), bf16),
            pltpu.VMEM((units, 2, group, width), bf16),
            pltpu.VMEM((units, 2, group, width), bf16),
            pltpu.VMEM((units, 2, group, width), bf16),
            pltpu.VMEM((chunks, 2, deep, width), bf16),
            pltpu.VMEM((4, chunks, 2, width), f32),
            pltpu.VMEM((2, 2, half), f32),
            pltpu.VMEM((8, rows), f32),
            pltpu.VMEM((8, cols), f32),
            pltpu.VMEM((8, 128), f32),
            pltpu.VMEM((2, deep, width), f32),
            pltpu.VMEM((2, deep, 128), f32),
            pltpu.VMEM((2, deep, 128), f32),
            pltpu.VMEM((2, 4, rows), f32),
            pltpu.VMEM((8, 4, rows), f32),
            pltpu.VMEM((8, 2, 128), f32),
            sem((6,)),
            sem((2, 4)),
            sem((4,)),
            sem((4,)),
            sem((7, 4)),
            sem((7, 4)),
            sem((6,)),
            sem((6,)),
            sem((8,)),
            sem((16,)),
            sem((8,)),
            sem((8,)),
            sem((16,)),
            sem((2,)),
            sem((chunks,)),
            sem((2,)),
            sem((3, 2)),
            sem((3, 8)),
            sem,
            sem,
            sem((7,)),
            sem((7,)),
            sem((7,)),
            sem((7,)),
            sem((3,)),
        ],
        compiler_params=pltpu.CompilerParams(
            collective_id=0, has_side_effects=True, vmem_limit_bytes=56 * 1024 * 1024
        ),
        name="block_step",
    )(
        pool,
        visible.reshape(1, -1),
        out_grad,
        ln_gain.reshape(1, -1),
        master_up,
        master_down,
        row_up,
        row_down,
        col_up.reshape(1, -1),
        col_down.reshape(1, -1),
    )
    return finish_all(grads, row_new, col_new, energy, depth * cols * 4)


def suits_block_step(pool, out_grad, master):
    rows, cols = master.shape
    tokens, depth = out_grad.shape
    return (
        lax.axis_size("dp") == 8
        and lax.axis_size("mp") == 4
        and rows * 8 == depth
        and rows % 64 == 0
        and cols % 256 == 0
        and cols >= 512
        and tokens % 64 == 0
        and pool.shape[0] % 16 == 0
    )


def on_device(
    token_pool,
    visible,
    out_grad,
    ln_gain,
    master_up,
    master_down,
    row_up,
    col_up,
    row_down,
    col_down,
):
    if suits_block_step(token_pool, out_grad, master_up):
        return block_step(
            token_pool,
            visible,
            out_grad,
            ln_gain,
            master_up,
            master_down,
            row_up,
            col_up,
            row_down,
            col_down,
        )
    picked = jnp.take(token_pool, visible, axis=0).astype(jnp.float32)
    normed = normalize(picked, ln_gain)
    grid_rows = master_up.shape[0]
    grid_cols = master_up.shape[1]
    depth = grid_rows * lax.axis_size("dp")
    breadth = grid_cols * lax.axis_size("mp")
    w_up = master_up.astype(jnp.bfloat16)
    w_down = master_down.astype(jnp.bfloat16)
    grad_up, grad_down = gathered_grads(normed, out_grad, w_up, w_down)
    squares_up = grad_up * grad_up + tiny_value
    squares_down = grad_down * grad_down + tiny_value
    rowpart_up = jnp.sum(squares_up, axis=1)
    rowpart_down = jnp.sum(squares_down, axis=1)
    colpart_up = jnp.sum(squares_up, axis=0)
    colpart_down = jnp.sum(squares_down, axis=0)
    rowsum_up, rowsum_down = lax.psum((rowpart_up, rowpart_down), "mp")
    colsum_up, colsum_down = lax.psum((colpart_up, colpart_down), "dp")
    row_up_new = decay_rate * row_up + (1.0 - decay_rate) * rowsum_up / breadth
    row_down_new = decay_rate * row_down + (1.0 - decay_rate) * rowsum_down / breadth
    col_up_new = decay_rate * col_up + (1.0 - decay_rate) * colsum_up / depth
    col_down_new = decay_rate * col_down + (1.0 - decay_rate) * colsum_down / depth
    raw_up = finish_update(grad_up, row_up_new, col_up_new)
    raw_down = finish_update(grad_down, row_down_new, col_down_new)
    energy_up, energy_down = lax.psum(
        (jnp.sum(raw_up * raw_up), jnp.sum(raw_down * raw_down)), ("dp", "mp")
    )
    update_up = raw_up / jnp.maximum(1.0, jnp.sqrt(energy_up / (depth * breadth)))
    update_down = raw_down / jnp.maximum(1.0, jnp.sqrt(energy_down / (depth * breadth)))
    return (update_up, update_down, row_up_new, col_up_new, row_down_new, col_down_new)


def solution(mesh):
    return jax.shard_map(
        on_device,
        mesh=mesh,
        in_specs=(
            P("dp", None),
            P("dp"),
            P("dp", None),
            P(),
            P("dp", "mp"),
            P("dp", "mp"),
            P("dp"),
            P("mp"),
            P("dp"),
            P("mp"),
        ),
        out_specs=(P("dp", "mp"), P("dp", "mp"), P("dp"), P("mp"), P("dp"), P("mp")),
        check_vma=False,
    )
```

```python
import functools
import jax
import jax.numpy as jnp
from jax import lax
from jax.experimental import pallas as pl
from jax.experimental.pallas import tpu as pltpu
from jax.sharding import PartitionSpec as P

decay_rate = 0.8
norm_eps = 1e-06
tiny_value = 1e-30


def gelu_tanh(values):
    return jax.nn.gelu(values, approximate=True)


def normalize(values, gain):
    mean_val = jnp.mean(values, axis=1, keepdims=True)
    centred = values - mean_val
    variance = jnp.mean(centred * centred, axis=1, keepdims=True)
    return (centred * lax.rsqrt(variance + norm_eps) * gain).astype(jnp.bfloat16)


def contract_tokens(left, right):
    return lax.dot_general(
        left, right, (((0,), (0,)), ((), ())), preferred_element_type=jnp.float32
    )


def finish_update(grad, row_new, col_new):
    return grad * lax.rsqrt(row_new[:, None] * col_new[None, :])


def gathered_grads(normed, out_grad, w_up, w_down):
    left = normed
    pre_act = jnp.dot(
        left, lax.all_gather(w_up, "dp", axis=0, tiled=True), preferred_element_type=jnp.float32
    )
    act_value, pull_back = jax.vjp(gelu_tanh, pre_act)
    hidden_act = act_value.astype(jnp.bfloat16)
    left = out_grad
    act_grad = jnp.dot(
        left, lax.all_gather(w_down, "dp", axis=0, tiled=True), preferred_element_type=jnp.float32
    )
    pre_grad = pull_back(act_grad)[0].astype(jnp.bfloat16)
    grad_down = lax.psum_scatter(
        contract_tokens(out_grad, hidden_act), "dp", scatter_dimension=0, tiled=True
    )
    grad_up = lax.psum_scatter(
        contract_tokens(normed, pre_grad), "dp", scatter_dimension=0, tiled=True
    )
    return grad_up, grad_down


MESH = pl.DeviceIdType.MESH


def flipped(index):
    return index + 1 - 2 * lax.rem(index, 2)


def greet(devices):
    barrier = pltpu.get_barrier_semaphore()
    for device in devices:
        pl.semaphore_signal(barrier, inc=1, device_id=device, device_id_type=MESH)
    pl.semaphore_wait(barrier, len(devices))


def send(src, dst, send_sem, recv_sem, device):
    return pltpu.make_async_remote_copy(
        src_ref=src,
        dst_ref=dst,
        send_sem=send_sem,
        recv_sem=recv_sem,
        device_id=device,
        device_id_type=MESH,
    )


def block_step_kernel(
    sizes,
    pool,
    visible,
    out_grad,
    gain,
    master_up,
    master_down,
    row_up,
    row_down,
    col_up,
    col_down,
    grads,
    row_new,
    col_new,
    energy,
    pool_buf,
    picked,
    means,
    scales,
    acts,
    left,
    left_t,
    masters,
    cast_out,
    weights,
    partial,
    crossing,
    hidden,
    grad_buf,
    col_parts,
    col_halves,
    row_buf,
    col_buf,
    sum_buf,
    begun,
    row_acc,
    spent_acc,
    stats,
    stat_buf,
    energy_buf,
    local_sem,
    master_sem,
    lev_send,
    lev_recv,
    act_send,
    act_recv,
    weight_send,
    weight_recv,
    part_send,
    part_recv,
    cross_recv,
    hid_send,
    hid_recv,
    grad_send,
    grad_recv,
    store_sem,
    col_send,
    col_recv,
    half_send,
    half_recv,
    stat_send,
    stat_recv,
    energy_send,
    energy_recv,
    out_sem,
):
    chunks, width, span, first_chunks, lag_inner, lag_outer = sizes
    me = lax.axis_index("dp")
    col = lax.axis_index("mp")
    z = lax.div(me, 2)
    y = lax.rem(me, 2)
    inner = jnp.logical_or(z == 1, z == 2)
    outer = jnp.logical_not(inner)
    rows = master_up.shape[0]
    half = master_up.shape[1] // 2
    depth = rows * 8
    breadth = master_up.shape[1] * 4
    deep = 2 * rows
    block = out_grad.shape[0]
    part = block // 4
    group = span * block
    groups = 8 // span
    units = chunks * groups
    joint = 2 // span
    mine = y * 4 + col
    beside = flipped(me)
    core = flipped(col)
    across = lax.rem(col + 2, 4)
    near = jnp.where(z < 2, 1, 2)
    inward = me + jnp.where(z < 2, 2, -2)
    outward = me - jnp.where(z < 2, 2, -2)
    masters_in = (master_up, master_down)
    peers = [lax.rem(me + shift, 8) for shift in range(1, 8)]
    level = [lax.rem(mine + shift, 8) for shift in range(1, 8)]
    barrier = pltpu.get_barrier_semaphore()
    greeted = (
        [(other, col) for other in peers]
        + [(me, lax.rem(col + shift, 4)) for shift in range(1, 4)]
        + [(beside, lax.rem(col + shift, 4)) for shift in range(1, 4)]
    )
    for device in greeted:
        pl.semaphore_signal(barrier, inc=1, device_id=device, device_id_type=MESH)

    def place(owner):
        return jnp.where(owner == 0, 2, jnp.where(owner == 1, 0, jnp.where(owner == 2, 1, 3)))

    def level_device(index):
        return (z * 2 + lax.div(index, 4), lax.rem(index, 4))

    def cut(index, size):
        return pl.ds(pl.multiple_of(index * size, size), size)

    pool_loads = []
    for at in range(4):
        cols = pl.ds(at * deep, deep)
        pool_loads.append(pltpu.make_async_copy(pool.at[:, cols], pool_buf.at[:, cols], local_sem.at[2 + at]))
    load_out = pltpu.make_async_copy(out_grad.at[cut(col, part)], acts.at[1], local_sem.at[1])

    load_mine = pltpu.make_async_copy(
        out_grad.at[:, cut(z, deep)], left.at[1, cut(place(z), block)], local_sem.at[0]
    )

    def master_loads(late):
        copies = []
        for a in range(2):
            for side in range(2):
                owner = y if side == 0 else 1 - y
                start = pl.multiple_of(owner * half + late * first_chunks * width, width)
                cols = pl.ds(start, half - first_chunks * width if late else first_chunks * width)
                copies.append(
                    pltpu.make_async_copy(
                        masters_in[a].at[:, cols], masters.at[a, :, cols], master_sem.at[late, 2 * a + side]
                    )
                )
        return copies

    for load in pool_loads:
        load.start()
    load_out.start()
    load_mine.start()

    my_rows = cut(y, rows)
    their_rows = cut(1 - y, rows)

    def weight_copy(k):
        return send(
            cast_out.at[k],
            weights.at[k, :, my_rows],
            weight_send.at[lax.rem(k, 6)],
            weight_recv.at[lax.rem(k, 6)],
            (beside, col),
        )

    def strip(owner, k):
        return pl.ds(pl.multiple_of(owner * half + k * width, width), width)

    def cast_theirs(k):
        for a in range(2):
            cast_out[k, a] = masters[a, :, strip(1 - y, k)].astype(jnp.bfloat16)
        weight_copy(k).start()

    def cast_mine(k):
        for a in range(2):
            weights[k, a, my_rows] = masters[a, :, strip(y, k)].astype(jnp.bfloat16)

    places = lax.broadcasted_iota(jnp.int32, (pool.shape[0], block), 0)
    chosen = (places == visible[...]).astype(jnp.bfloat16)
    for level_at, load in enumerate(pool_loads):
        load.wait()
        at = pl.ds(level_at * deep, deep)
        picked[:, at] = contract_tokens(chosen, pool_buf[:, at])
        if level_at == 1:
            for copy in master_loads(0):
                copy.start()
    values = picked[...]
    mean_val = jnp.mean(values, axis=1, keepdims=True)
    centred = values - mean_val
    variance = jnp.mean(centred * centred, axis=1, keepdims=True)
    means[...] = mean_val
    scales[...] = lax.rsqrt(variance + norm_eps)

    def normed_at(some, at):
        shifted = picked[some, at] - means[some]
        return (shifted * scales[some] * gain[:, at]).astype(jnp.bfloat16)

    acts[0] = normed_at(cut(col, part), pl.ds(0, depth))
    left[0, cut(place(z), block)] = normed_at(pl.ds(0, block), cut(z, deep))
    load_out.wait()
    load_mine.wait()
    pl.semaphore_wait(barrier, len(greeted))

    first = jnp.where(inner, 3 - z, near)
    second = jnp.where(inner, jnp.where(z == 1, 0, 3), 3 - near)
    third = jnp.where(z < 2, 3, 0)
    owners = [z, first, second, third]
    spots = [place(owner) for owner in owners]

    def piece(spot, quarter):
        return left.at[:, pl.ds(pl.multiple_of(spot * block + quarter * part, part), part)]

    def lev_copy(to, source):
        return send(
            acts.at[:, :, cut(to, deep)],
            piece(place(source), col),
            lev_send.at[to],
            lev_recv.at[source],
            (to * 2 + y, col),
        )

    def lev_start():
        for to in owners[1:]:
            lev_copy(to, z).start()

    def share(kind, at, src, dst, quarter, device):
        return send(
            piece(src, quarter), piece(dst, quarter), act_send.at[kind, at], act_recv.at[kind, at], device
        )

    def along_x(at):
        return share(0, at, at, at, col, (me, across))

    def along_y(at):
        return share(1, at, at, 4 + at, col, (beside, col))

    def turned(at):
        return share(2, at, 4 + at, 4 + at, col, (me, across))

    def to_core(at, far, quarter):
        spot = at + 4 * far
        return share(3 + 2 * far + quarter, at, spot, spot, across if quarter else col, (me, core))

    def spread_out(at):
        along_x(at).start()
        along_y(at).start()
        to_core(at, 0, 0).start()

    def crossed_x(at):
        along_x(at).wait_recv()
        to_core(at, 0, 1).start()

    def crossed_y(index):
        at = spots[index]
        along_y(at).wait_recv()
        turned(at).start()
        to_core(at, 1, 0).start()

    def crossed_both(index):
        turned(spots[index]).wait_recv()
        to_core(spots[index], 1, 1).start()

    def ready(spot):
        for quarter in range(2):
            to_core(spot % 4, spot // 4, quarter).wait_recv()

    def arrive(index):
        lev_copy(owners[index], owners[index]).wait_recv()
        spread_out(spots[index])

    along_y(spots[0]).start()

    @pl.when(inner)
    def _():
        lev_start()

    for copy in master_loads(0):
        copy.wait()
    for k in range(first_chunks):
        cast_theirs(k)
    for k in range(first_chunks):
        cast_mine(k)
    row_acc[...] = jnp.zeros_like(row_acc)
    spent_acc[...] = jnp.zeros_like(spent_acc)
    lev_copy(first, first).wait_recv()

    @pl.when(outer)
    def _():
        lev_start()

    spread_out(spots[1])
    for copy in master_loads(1):
        copy.start()

    def run(steps):
        for step, index in steps:
            step(index)

    def cross_x(index):
        crossed_x(spots[index])

    outer_steps = {
        0: [(crossed_y, 0), (arrive, 2), (cross_x, 1), (cross_x, 2)],
        1: [(arrive, 3), (crossed_both, 0)],
    }
    inner_steps = {
        0: [(crossed_y, 0), (cross_x, 1), (arrive, 2), (arrive, 3), (crossed_both, 0), (cross_x, 2)],
        1: [],
    }
    both = {
        2: [(cross_x, 3), (crossed_y, 1)],
        3: [(crossed_y, 2), (crossed_y, 3), (crossed_both, 1)],
        4: [(crossed_both, 2)],
        5: [(crossed_both, 3)],
    }

    @pl.when(outer)
    def _():
        run(outer_steps[0])

    @pl.when(inner)
    def _():
        run(inner_steps[0])

    def part_copy(u, step, to_peer):
        recv = cross_recv if to_peer else part_recv
        return send(
            partial.at[u],
            (crossing if to_peer else partial).at[u],
            part_send.at[lax.rem(step, 8)],
            recv.at[lax.rem(step, recv.shape[0])],
            (inward, col),
        )

    def hid_copy(u, step):
        return send(
            hidden.at[u],
            hidden.at[u],
            hid_send.at[lax.rem(step, 8)],
            hid_recv.at[lax.rem(step, hid_recv.shape[0])],
            (outward, col),
        )

    def grad_cols(k):
        return pl.ds(pl.multiple_of(y * half + k * width, width), width)

    def grad_copy(k):
        return send(
            grad_buf.at[k, :, their_rows],
            grads.at[:, :, grad_cols(k)],
            grad_send.at[lax.rem(k, 2)],
            grad_recv.at[k],
            (beside, col),
        )

    def grad_store(k):
        return pltpu.make_async_copy(
            grad_buf.at[k, :, my_rows], grads.at[:, :, grad_cols(k)], store_sem.at[lax.rem(k, 2)]
        )

    def col_copies(k):
        copies = []
        for shift in range(1, 4):
            copies.append(
                send(
                    col_parts.at[z, k],
                    col_parts.at[z, k],
                    col_send.at[shift - 1, lax.rem(k, 2)],
                    col_recv.at[shift - 1, lax.rem(k, 8)],
                    (lax.rem(z + shift, 4) * 2 + y, col),
                )
            )
        return copies

    def unit(step):
        early = step < first_chunks * groups
        pair = lax.div(step, joint)
        k = jnp.where(early, lax.rem(pair, first_chunks), lax.div(step, groups))
        g = jnp.where(
            early,
            lax.div(pair, first_chunks) * joint + lax.rem(step, joint),
            lax.rem(step, groups),
        )
        return k, g, k * groups + g

    def multiply(step):
        k, g, u = unit(step)

        @pl.when(step >= 8)
        def _():
            part_copy(u, step, False).wait_send()

        @pl.when(jnp.logical_and(g == groups // 2, jnp.logical_and(k + 2 >= first_chunks, k + 2 < chunks)))
        def _():
            @pl.when(k >= 4)
            def _():
                weight_copy(k - 4).wait_send()

            cast_theirs(k + 2)
            cast_mine(k + 2)

        @pl.when(g == 0)
        def _():
            weight_copy(k).wait_recv()

        spot = cut(g, group)
        sums = [
            jnp.dot(left[a, spot], weights[k, a], preferred_element_type=jnp.float32) for a in range(2)
        ]

        @pl.when(outer)
        def _():
            for a in range(2):
                partial[u, a] = sums[a].astype(jnp.bfloat16)
            part_copy(u, step, False).start()

        @pl.when(inner)
        def _():
            part_copy(u, step, False).wait_recv()
            for a in range(2):
                partial[u, a] = (partial[u, a].astype(jnp.float32) + sums[a]).astype(jnp.bfloat16)
            part_copy(u, step, True).start()

        @pl.when(k == 0)
        def _():
            for a in range(2):
                left_t[a, :, spot] = left[a, spot].T

    def activate(u, step):
        part_copy(u, step, True).wait_recv()
        pre_act, act_grad = [
            partial[u, a].astype(jnp.float32) + crossing[u, a].astype(jnp.float32) for a in range(2)
        ]
        scale = 0.7978845608028654
        square = pre_act * pre_act
        bent = jnp.tanh(scale * (pre_act + 0.044715 * (square * pre_act)))
        lift = 0.5 * (1.0 + bent)
        slope = lift + 0.5 * pre_act * (1.0 - bent * bent) * (scale * (1.0 + 3 * 0.044715 * square))
        hidden[u, 0] = (act_grad * slope).astype(jnp.bfloat16)
        hidden[u, 1] = (pre_act * lift).astype(jnp.bfloat16)
        hid_copy(u, step).start()

    def fold(values):
        lanes = values[:, :128]
        for at in range(128, width, 128):
            lanes += values[:, at : at + 128]
        return lanes

    def finish_cols(k):
        for copy in col_copies(k):
            copy.wait_recv()
        total = col_parts[0, k] + col_parts[1, k] + col_parts[2, k] + col_parts[3, k]
        at = pl.multiple_of(k * width, width)
        for a, old in enumerate((col_up, col_down)):
            kept = old[:, pl.ds(pl.multiple_of(y * half + at, width), width)]
            fresh = decay_rate * kept + (1.0 - decay_rate) * total[a : a + 1] / depth
            col_halves[y, a : a + 1, pl.ds(at, width)] = fresh
            inverse = 1.0 / fresh
            for side in range(2):
                strip = pl.ds(side * rows, rows)
                grad = grad_buf[k, a, strip].astype(jnp.float32)
                spent_acc[a, strip] += fold(grad * grad * inverse)

    def grad_part(k, a, strip, g):
        return jnp.dot(
            left_t[a, strip, pl.ds(g * group, group)],
            hidden[k * groups + g, a],
            preferred_element_type=jnp.float32,
        )

    def begin_chunk(k):
        for a in range(2):
            for side in range(2):
                strip = pl.ds(side * rows, rows)
                grad = grad_part(k, a, strip, 0)
                for g in range(1, groups - 1):
                    grad += grad_part(k, a, strip, g)
                begun[a, strip] = grad

    def finish_chunk(k):
        for a in range(2):
            total = jnp.zeros((1, width), jnp.float32)
            for side in range(2):
                strip = pl.ds(side * rows, rows)
                grad = begun[a, strip] + grad_part(k, a, strip, groups - 1)
                grad_buf[k, a, strip] = grad.astype(jnp.bfloat16)
                squares = grad * grad + tiny_value
                total += jnp.sum(squares, axis=0, keepdims=True)
                row_acc[a, strip] += fold(squares)
            col_parts[z, k, a : a + 1] = total
        @pl.when(k >= 2)
        def _():
            for copy in col_copies(k):
                copy.wait_send()
            grad_copy(k).wait_send()
            grad_store(k).wait()

        for copy in col_copies(k):
            copy.start()
        grad_copy(k).start()
        grad_store(k).start()

        @pl.when(k > 2)
        def _():
            finish_cols(k - 3)

    behind = jnp.where(inner, lag_inner, lag_outer)

    @pl.loop(0, units + lag_outer)
    def _(s):
        @pl.when(jnp.logical_and(s == 1, outer))
        def _():
            run(outer_steps[1])

        @pl.when(s == 0)
        def _():
            for copy in master_loads(1):
                copy.wait()

        for at in both:
            @pl.when(s == at * 2 // span)
            def _():
                run(both[at])

        for pair in range(4):
            @pl.when(s == pair * joint * first_chunks)
            def _():
                for spot in range(2 * pair, 2 * pair + 2):
                    if spot < 4:
                        @pl.when(spots[0] != spot)
                        def _():
                            ready(spot)
                    else:
                        ready(spot)

        @pl.when(s < units)
        def _():
            multiply(s)

        v = s - behind

        @pl.when(jnp.logical_and(v >= 0, v < units))
        def _():
            k, g, u = unit(v)

            @pl.when(jnp.logical_and(inner, v >= 8))
            def _():
                hid_copy(u, v).wait_send()

            @pl.when(inner)
            def _():
                activate(u, v)

            @pl.when(outer)
            def _():
                hid_copy(u, v).wait_recv()

            @pl.when(g == groups - 2)
            def _():
                begin_chunk(k)

            @pl.when(g == groups - 1)
            def _():
                finish_chunk(k)

    def put_lines(place_at, source):
        for a in range(2):
            line = jnp.sum(source[a].T, axis=0, keepdims=True)
            for owner in range(2):
                stats[owner, place_at + a : place_at + a + 1] = line[:, owner * rows : (owner + 1) * rows]

    put_lines(0, row_acc)
    for k in range(chunks - 3, chunks):
        finish_cols(k)
    put_lines(2, spent_acc)
    stat_buf[mine] = stats[y]
    stat_copies = []
    for shift in range(1, 8):
        to = level[shift - 1]
        copy = send(
            stats.at[lax.div(to, 4)],
            stat_buf.at[mine],
            stat_send.at[shift - 1],
            stat_recv.at[shift - 1],
            level_device(to),
        )
        copy.start()
        stat_copies.append(copy)
    half_copy = send(col_halves.at[y], col_halves.at[y], half_send, half_recv, (beside, col))
    half_copy.start()
    for copy in stat_copies:
        copy.wait_recv()
    total = stat_buf[0]
    for source in range(1, 8):
        total = total + stat_buf[source]
    for a, old in enumerate((row_up, row_down)):
        fresh = decay_rate * old[...].reshape(1, rows) + (1.0 - decay_rate) * total[a : a + 1] / breadth
        row_buf[a : a + 1] = fresh
        spent = jnp.sum(total[2 + a : 3 + a] / fresh, axis=1, keepdims=True)
        energy_buf[me, a : a + 1] = jnp.broadcast_to(spent, (1, 128))
    energy_copies = []
    for shift, other in enumerate(peers):
        copy = send(
            energy_buf.at[me], energy_buf.at[me], energy_send.at[shift], energy_recv.at[shift], (other, col)
        )
        copy.start()
        energy_copies.append(copy)
    row_out = pltpu.make_async_copy(row_buf, row_new, out_sem.at[0])
    row_out.start()
    half_copy.wait_recv()
    for owner in range(2):
        col_buf[0:2, owner * half : (owner + 1) * half] = col_halves[owner]
    col_out = pltpu.make_async_copy(col_buf, col_new, out_sem.at[1])
    col_out.start()

    for shift in range(1, 4):
        lev_copy(lax.rem(z + shift, 4), z).wait_send()
    for at in range(4):
        for copy in [along_y(at), turned(at), to_core(at, 1, 0), to_core(at, 1, 1)]:
            copy.wait_send()

        @pl.when(spots[0] != at)
        def _():
            for copy in [along_x(at), to_core(at, 0, 0), to_core(at, 0, 1)]:
                copy.wait_send()

    @pl.loop(0, 8)
    def _(slot):
        part_copy(slot, slot, False).wait_send()

        @pl.when(inner)
        def _():
            hid_copy(slot, slot).wait_send()

    @pl.loop(0, chunks)
    def _(k):
        grad_copy(k).wait_recv()

        @pl.when(k >= chunks - 2)
        def _():
            grad_copy(k).wait_send()
            grad_store(k).wait()
            for copy in col_copies(k):
                copy.wait_send()

        @pl.when(k >= chunks - 6)
        def _():
            weight_copy(k).wait_send()

    for copy in energy_copies:
        copy.wait_recv()
    summed = energy_buf[0]
    for source in range(1, 8):
        summed = summed + energy_buf[source]
    sum_buf[0:2] = summed
    sum_out = pltpu.make_async_copy(sum_buf, energy, out_sem.at[2])
    sum_out.start()
    row_out.wait()
    col_out.wait()
    sum_out.wait()
    for copy in [half_copy] + stat_copies + energy_copies:
        copy.wait_send()


def scale_kernel(count, size, grads, row_new, col_new, energy, *refs):
    updates, line_outs = refs[:2], refs[2:6]
    out_buf, line_bufs, store_sem, line_sem = refs[6], refs[7:11], refs[11], refs[12]
    stores = []
    for at, (source, a) in enumerate(((row_new, 0), (row_new, 1), (col_new, 0), (col_new, 1))):
        line_bufs[at][...] = source[a, :]
        stores.append(pltpu.make_async_copy(line_bufs[at], line_outs[at], line_sem.at[at]))
        stores[-1].start()
    shrink = jnp.maximum(1.0, jnp.sqrt(energy[...] / count))
    upright = (lax.rsqrt(row_new[...]) / shrink[:, 0:1]).T
    cols = lax.rsqrt(col_new[...])
    for at in range(grads.shape[1] // size):
        span = pl.ds(at * size, size)
        for a in range(2):
            tall = upright[at * size : (at + 1) * size, a : a + 1]
            out_buf[a, span] = grads[a, span].astype(jnp.float32) * tall * cols[a : a + 1]
            stores.append(
                pltpu.make_async_copy(out_buf.at[a, span], updates[a].at[span], store_sem.at[a, at])
            )
            stores[-1].start()
    for store in stores:
        store.wait()


def finish_all(grads, row_new, col_new, energy, count):
    rows, cols = grads.shape[1:]
    size = 64
    f32 = jnp.float32
    update = jax.ShapeDtypeStruct((rows, cols), f32)
    line = jax.ShapeDtypeStruct((rows,), f32)
    wide = jax.ShapeDtypeStruct((cols,), f32)
    anywhere = pl.BlockSpec(memory_space=pl.ANY)
    vmem = pl.BlockSpec(memory_space=pltpu.VMEM)
    outs = pl.pallas_call(
        functools.partial(scale_kernel, count, size),
        out_shape=(update, update, line, line, wide, wide),
        in_specs=[vmem] * 4,
        out_specs=(anywhere,) * 6,
        scratch_shapes=[
            pltpu.VMEM(grads.shape, f32),
            pltpu.VMEM((rows,), f32),
            pltpu.VMEM((rows,), f32),
            pltpu.VMEM((cols,), f32),
            pltpu.VMEM((cols,), f32),
            pltpu.SemaphoreType.DMA((2, rows // size)),
            pltpu.SemaphoreType.DMA((4,)),
        ],
        compiler_params=pltpu.CompilerParams(vmem_limit_bytes=24 * 1024 * 1024),
        cost_estimate=pl.CostEstimate(
            flops=4 * rows * cols, bytes_accessed=12 * rows * cols, transcendentals=0
        ),
        name="scale",
    )(grads, row_new, col_new, energy)
    return (outs[0], outs[1], outs[2], outs[4], outs[3], outs[5])


def block_step(pool, visible, out_grad, ln_gain, master_up, master_down, row_up, col_up, row_down, col_down):
    rows, cols = master_up.shape
    tokens, depth = out_grad.shape
    half = cols // 2
    width = 128
    span = 1
    chunks = half // width
    groups = 8 // span
    units = chunks * groups
    deep, part = 2 * rows, tokens // 4
    group = span * tokens
    f32, bf16 = jnp.float32, jnp.bfloat16
    anywhere = pl.BlockSpec(memory_space=pl.ANY)
    vmem = pl.BlockSpec(memory_space=pltpu.VMEM)
    sem = pltpu.SemaphoreType.DMA
    grads, row_new, col_new, energy = pl.pallas_call(
        functools.partial(block_step_kernel, (chunks, width, span, 2, 3, 14)),
        out_shape=(
            pltpu.VMEM((2, rows, cols), bf16),
            pltpu.VMEM((8, rows), f32),
            pltpu.VMEM((8, cols), f32),
            pltpu.VMEM((8, 128), f32),
        ),
        in_specs=[anywhere, vmem, anywhere, vmem, anywhere, anywhere, vmem, vmem, vmem, vmem],
        out_specs=(vmem,) * 4,
        scratch_shapes=[
            pltpu.VMEM(pool.shape, bf16),
            pltpu.VMEM(out_grad.shape, f32),
            pltpu.VMEM((tokens, 1), f32),
            pltpu.VMEM((tokens, 1), f32),
            pltpu.VMEM((2, part, depth), bf16),
            pltpu.VMEM((2, groups * group, deep), bf16),
            pltpu.VMEM((2, deep, groups * group), bf16),
            pltpu.VMEM((2, rows, cols), f32),
            pltpu.VMEM((chunks, 2, rows, width), bf16),
            pltpu.VMEM((chunks, 2, deep, width), bf16),
            pltpu.VMEM((units, 2, group, width), bf16),
            pltpu.VMEM((units, 2, group, width), bf16),
            pltpu.VMEM((units, 2, group, width), bf16),
            pltpu.VMEM((chunks, 2, deep, width), bf16),
            pltpu.VMEM((4, chunks, 2, width), f32),
            pltpu.VMEM((2, 2, half), f32),
            pltpu.VMEM((8, rows), f32),
            pltpu.VMEM((8, cols), f32),
            pltpu.VMEM((8, 128), f32),
            pltpu.VMEM((2, deep, width), f32),
            pltpu.VMEM((2, deep, 128), f32),
            pltpu.VMEM((2, deep, 128), f32),
            pltpu.VMEM((2, 4, rows), f32),
            pltpu.VMEM((8, 4, rows), f32),
            pltpu.VMEM((8, 2, 128), f32),
            sem((6,)),
            sem((2, 4)),
            sem((4,)),
            sem((4,)),
            sem((7, 4)),
            sem((7, 4)),
            sem((6,)),
            sem((6,)),
            sem((8,)),
            sem((16,)),
            sem((8,)),
            sem((8,)),
            sem((16,)),
            sem((2,)),
            sem((chunks,)),
            sem((2,)),
            sem((3, 2)),
            sem((3, 8)),
            sem,
            sem,
            sem((7,)),
            sem((7,)),
            sem((7,)),
            sem((7,)),
            sem((3,)),
        ],
        compiler_params=pltpu.CompilerParams(
            collective_id=0, has_side_effects=True, vmem_limit_bytes=56 * 1024 * 1024
        ),
        name="block_step",
    )(
        pool,
        visible.reshape(1, -1),
        out_grad,
        ln_gain.reshape(1, -1),
        master_up,
        master_down,
        row_up,
        row_down,
        col_up.reshape(1, -1),
        col_down.reshape(1, -1),
    )
    return finish_all(grads, row_new, col_new, energy, depth * cols * 4)


def suits_block_step(pool, out_grad, master):
    rows, cols = master.shape
    tokens, depth = out_grad.shape
    return (
        lax.axis_size("dp") == 8
        and lax.axis_size("mp") == 4
        and rows * 8 == depth
        and rows % 64 == 0
        and cols % 256 == 0
        and cols >= 512
        and tokens % 64 == 0
        and pool.shape[0] % 16 == 0
    )


def on_device(
    token_pool,
    visible,
    out_grad,
    ln_gain,
    master_up,
    master_down,
    row_up,
    col_up,
    row_down,
    col_down,
):
    if suits_block_step(token_pool, out_grad, master_up):
        return block_step(
            token_pool,
            visible,
            out_grad,
            ln_gain,
            master_up,
            master_down,
            row_up,
            col_up,
            row_down,
            col_down,
        )
    picked = jnp.take(token_pool, visible, axis=0).astype(jnp.float32)
    normed = normalize(picked, ln_gain)
    grid_rows = master_up.shape[0]
    grid_cols = master_up.shape[1]
    depth = grid_rows * lax.axis_size("dp")
    breadth = grid_cols * lax.axis_size("mp")
    w_up = master_up.astype(jnp.bfloat16)
    w_down = master_down.astype(jnp.bfloat16)
    grad_up, grad_down = gathered_grads(normed, out_grad, w_up, w_down)
    squares_up = grad_up * grad_up + tiny_value
    squares_down = grad_down * grad_down + tiny_value
    rowpart_up = jnp.sum(squares_up, axis=1)
    rowpart_down = jnp.sum(squares_down, axis=1)
    colpart_up = jnp.sum(squares_up, axis=0)
    colpart_down = jnp.sum(squares_down, axis=0)
    rowsum_up, rowsum_down = lax.psum((rowpart_up, rowpart_down), "mp")
    colsum_up, colsum_down = lax.psum((colpart_up, colpart_down), "dp")
    row_up_new = decay_rate * row_up + (1.0 - decay_rate) * rowsum_up / breadth
    row_down_new = decay_rate * row_down + (1.0 - decay_rate) * rowsum_down / breadth
    col_up_new = decay_rate * col_up + (1.0 - decay_rate) * colsum_up / depth
    col_down_new = decay_rate * col_down + (1.0 - decay_rate) * colsum_down / depth
    raw_up = finish_update(grad_up, row_up_new, col_up_new)
    raw_down = finish_update(grad_down, row_down_new, col_down_new)
    energy_up, energy_down = lax.psum(
        (jnp.sum(raw_up * raw_up), jnp.sum(raw_down * raw_down)), ("dp", "mp")
    )
    update_up = raw_up / jnp.maximum(1.0, jnp.sqrt(energy_up / (depth * breadth)))
    update_down = raw_down / jnp.maximum(1.0, jnp.sqrt(energy_down / (depth * breadth)))
    return (update_up, update_down, row_up_new, col_up_new, row_down_new, col_down_new)


def solution(mesh):
    return jax.shard_map(
        on_device,
        mesh=mesh,
        in_specs=(
            P("dp", None),
            P("dp"),
            P("dp", None),
            P(),
            P("dp", "mp"),
            P("dp", "mp"),
            P("dp"),
            P("mp"),
            P("dp"),
            P("mp"),
        ),
        out_specs=(P("dp", "mp"), P("dp", "mp"), P("dp"), P("mp"), P("dp"), P("mp")),
        check_vma=False,
    )
```
